32 devices in a mesh: store: 8 (over z, y), tensor: 4 (over x, core).
Axes of the slice: x: 2, y: 2, z: 4, core: 2. Of those that a mesh axis runs over, the one named last changes fastest.
Arguments:
- tokens: bfloat16 [8192, 8192], P('store', 'tensor'), may hold values from -1200 to 1200
- norm_gain: float32 [8192], P('tensor'), may hold values from 0.1 to 1.9
- kv_weight: bfloat16 [8192, 2, 1024], P('tensor'), may hold values from -0.0625 to 0.0625
- adapter_down: bfloat16 [32, 8192, 128], P('store', 'tensor'), may hold values from -0.0625 to 0.0625
- adapter_up: bfloat16 [32, 2, 64, 1024], P('store', None, None, 'tensor'), may hold values from -0.75 to 0.75
- token_adapters: int32 [8192, 1], P('store'), may hold values from 0 to 31; in each aligned block of 1024 rows (0 to 1023, 1024 to 2047, ...) at most 40 rows name the same one
- adapter_slot: int32 [32], replicated, may hold values from 0 to 31, each once
- request_lengths: int32 [16], replicated, may hold values from 1 to 4096, 8192 in all
Outputs:
- new_keys: bfloat16 [8192, 1024], P('store', 'tensor')
- new_values: bfloat16 [8192, 1024], P('store', 'tensor')
The draws below stay inside these ranges and needn't reach their ends.
Inputs may be any that keep to these rules, and one draw needn't show every extreme that they name: `token_adapters`: among the 1024 tokens of one index of store no adapter is named more than 40 times; in every draw some adapter is named exactly 40 times by the tokens of some index. `adapter_slot`: each row 0 to 31 appears once. `request_lengths`: the lengths sum to 8192; the largest is exactly 4096.
All inputs are finite; a program needn't handle non-finite values.
Results may differ from the reference program's by a relative error of at most 0.0061.
Values may be sent and summed in bfloat16 or wider, within the bound.
A program may use at most 128 MiB of HBM per device.

```python
import math
import jax
import jax.numpy as jnp
import numpy as np
from jax import lax

D = 8192
KV = 1024
HEAD = 128
ADAPTER_RANK = 64
TOK_DEV = 1024
ADAPTER_COUNT = 32
TOKENS = 8192
TOKENS_PER_ADAPT = 40
REQS = 16
REQ_MOST = 4096
N_STORE = 8


def draw_tokens(key, part):
    column_key = jax.random.fold_in(key, 11)
    row_key = jax.random.fold_in(key, 23)
    value_key = jax.random.fold_in(key, 37)
    columns = jnp.arange(D, dtype=jnp.float32)
    column_scale = jnp.exp(math.log(3.0) * columns / (D - 1) + math.log(10.0) * jax.random.uniform(column_key, (D,), jnp.float32))
    row_scale = jnp.exp(math.log(10.0) * jax.random.uniform(row_key, (TOKENS, 1), jnp.float32))
    values = jax.random.truncated_normal(value_key, -4.0, 4.0, (TOKENS, D), jnp.float32)
    return (values * column_scale[None, :] * row_scale).astype(jnp.bfloat16)


def levels(own_key, shape, shards, smallest, high):
    gain, own = 1.0, jax.random.fold_in(own_key, 6)
    for position, blocks in shards:
        heights = jnp.exp(jax.random.uniform(jax.random.fold_in(own, position), (blocks,), jnp.float32, smallest / len(shards), high / len(shards)))
        gain = gain * jnp.repeat(heights, shape[position] // blocks).reshape([-1 if axis == position else 1 for axis in range(len(shape))])
    return gain


def split_up(number_of, total, limit, lean):
    portions = [(1 << 20) // math.isqrt(rank ** lean) + 1 for rank in range(2, number_of + 1)]
    surplus, holding = total - limit - (number_of - 1), [1] * (number_of - 1)
    while surplus > 0:
        free = [i for i in range(number_of - 1) if holding[i] < limit]
        pool, remaining = sum([portions[i] for i in free]), surplus
        for i in free:
            extra = min(limit - holding[i], max(1, remaining * portions[i] // pool), surplus)
            holding[i] = holding[i] + extra
            surplus = surplus - extra
    return np.array([limit] + holding)


def ragged_sizes(own_key, count, total, limit, slope):
    if count == 2:
        one = jax.random.randint(own_key, (), max(1, total - limit), min(limit, total - 1) + 1)
        return jnp.stack([one, total - one])
    sizes = jnp.asarray(split_up(count, total, limit, slope), jnp.int32)
    twos = (count - 1) // 2
    giver, receiver = sizes[1:1 + 2 * twos:2], sizes[2:2 + 2 * twos:2]
    slack = jnp.minimum(giver - 1, limit - receiver)
    passed = jax.random.randint(jax.random.fold_in(own_key, 1), (twos,), 0, 1 << 20) % (slack + 1)
    sizes = sizes.at[1:1 + 2 * twos:2].set(giver - passed).at[2:2 + 2 * twos:2].set(receiver + passed)
    return sizes[jax.random.permutation(jax.random.fold_in(own_key, 2), count)]


def assign_block(own_key, own, number, rows, number_of, top, limit, slope):
    sequence = jax.random.permutation(own_key, number_of)
    heavy_load, usual = load_shares(number_of, rows * top, limit, slope, True), load_shares(number_of, rows * top, limit, slope, False)
    places = jnp.arange(number_of)

    def named(sizes, turn):
        used = int((sizes > 0).sum())
        fixed = max(1, used // 4)
        moved = fixed + (places - fixed + turn * (used - fixed)) % max(1, number_of - fixed)
        return jnp.zeros((number_of,), jnp.int32).at[sequence[jnp.where(places < fixed, places, moved)]].set(jnp.asarray(sizes, jnp.int32))

    sizes = jnp.where(number % 4 == 0, named(heavy_load, number // 4), named(usual, number - number // 4 - 1))
    mixed = jax.random.permutation(jax.random.fold_in(own, 3), number_of)
    donor, sink = mixed[0:number_of // 2 * 2:2], mixed[1:number_of // 2 * 2:2]
    margin = jnp.minimum(sizes[donor] - 1, limit - sizes[sink]) // 2
    margin = jnp.where((donor == sequence[0]) | (sink == sequence[0]) | (sizes[sink] == 0), 0, jnp.maximum(margin, 0))
    moved = jax.random.randint(jax.random.fold_in(own, 4), (number_of // 2,), 0, 1 << 20) % (margin + 1)
    sizes = sizes.at[donor].add(-moved).at[sink].add(moved)
    members = jnp.searchsorted(jnp.cumsum(sizes), jnp.arange(rows * top), side="right").astype(jnp.int32)
    table = members.reshape(top, rows).T
    table = table[jax.random.permutation(jax.random.fold_in(own, 1), rows)]
    turn = jax.random.randint(jax.random.fold_in(own, 2), (rows, 1), 0, top)
    return jnp.take_along_axis(table, (jnp.arange(top)[None, :] + turn) % top, axis=1)


def load_shares(number_of, total, reach, lean, full):
    portions = [(1 << 20) // math.isqrt(rank ** lean) + 1 for rank in range(1, number_of + 1)]
    largest = reach if full else min(reach, max(-(-total // number_of), total * portions[0] // sum(portions)))
    least = 1 if total - largest >= number_of - 1 else 0
    counts, surplus = [largest] + [least] * (number_of - 1), total - largest - least * (number_of - 1)
    while surplus > 0:
        candidates = [i for i in range(1, number_of) if counts[i] < largest] or [i for i in range(1, number_of) if counts[i] < reach]
        pool, left = sum([portions[i] for i in candidates]), surplus
        for i in candidates:
            more = min(reach - counts[i], max(1, left * portions[i] // pool), surplus)
            counts[i] = counts[i] + more
            surplus = surplus - more
    return np.array(counts)


def centred(rng, extent, spread, most, pieces=(), kind=jnp.bfloat16):
    drawn = jax.random.normal(rng, extent, jnp.float32) * spread
    if len(pieces) > 0:
        drawn = levels(rng, extent, pieces, -0.22, 0.18) * drawn
    return jnp.clip(drawn, min=-most, max=most).astype(kind)


def setup_inputs(seed: int = 0) -> dict:
    key_of = jax.random.split(jax.random.key(seed), 9)
    tokens = draw_tokens(jax.random.fold_in(key_of[8], 71), 0)
    norm_gain = jnp.clip(1.0 + 0.18 * jax.random.normal(key_of[1], (D,), jnp.float32), 0.1, 1.9)
    kv_weight = centred(key_of[2], (D, 2, KV), D ** -0.5, 0.0625, ((0, 4),))
    adapter_down = centred(key_of[3], (ADAPTER_COUNT, D, 2 * ADAPTER_RANK), D ** -0.5, 0.0625, ((0, 8), (1, 4)))
    adapter_up = centred(key_of[4], (ADAPTER_COUNT, 2, ADAPTER_RANK, KV), ADAPTER_RANK ** -0.5, 0.75, ((0, 8), (3, 4)))
    token_adapters_keys = jax.random.split(jax.random.fold_in(key_of[5], 1), TOKENS // TOK_DEV)
    token_adapters_turns = jax.random.permutation(jax.random.fold_in(key_of[5], 3), TOKENS // TOK_DEV)
    token_adapters = jax.vmap(lambda own, number: assign_block(jax.random.fold_in(key_of[5], 2), own, number, TOK_DEV, ADAPTER_COUNT, 1, TOKENS_PER_ADAPT, 2))(token_adapters_keys, token_adapters_turns).reshape((TOKENS, 1))
    adapter_slot = jax.random.permutation(key_of[6], ADAPTER_COUNT).astype(jnp.int32)
    request_lengths = ragged_sizes(key_of[7], REQS, TOKENS, REQ_MOST, 2).astype(jnp.int32)
    return dict(tokens=tokens, norm_gain=norm_gain, kv_weight=kv_weight, adapter_down=adapter_down, adapter_up=adapter_up, token_adapters=token_adapters, adapter_slot=adapter_slot, request_lengths=request_lengths)


epsilon = 1e-05
adapter_scale = 2.0
rope_theta = 500000.0

def place_rows(adapter_ids, adapter_slot, capacity):
    catalog = jnp.arange(adapter_slot.shape[0], dtype=jnp.int32)
    slot_rows = lax.optimization_barrier(jnp.sum(jnp.where(adapter_ids[:, None] == catalog[None, :], adapter_slot[None, :], 0), axis=1)).astype(jnp.int32)
    row_order = jnp.arange(adapter_ids.shape[0], dtype=jnp.int32)
    same_earlier = (adapter_ids[:, None] == adapter_ids[None, :]) & (row_order[None, :] < row_order[:, None])
    rank_rows = lax.optimization_barrier(jnp.sum(same_earlier.astype(jnp.int32), axis=1)).astype(jnp.int32)
    return (slot_rows * capacity + rank_rows).astype(jnp.int32)

def positions_of(first_row, row_count, lengths):
    global_rows = first_row + jnp.arange(row_count, dtype=jnp.int32)
    request_ends = jnp.cumsum(lengths).astype(jnp.int32)
    preceding = lax.optimization_barrier(jnp.sum(jnp.where(request_ends[None, :] <= global_rows[:, None], lengths[None, :], 0), axis=1)).astype(jnp.int32)
    return (global_rows - preceding).astype(jnp.int32)

def rotate(states, positions):
    per_head = states.reshape(states.shape[0], -1, HEAD)
    half_size = HEAD // 2
    frequency = jnp.exp(jnp.arange(half_size, dtype=jnp.float32) * (-2.0 * math.log(rope_theta) / HEAD))
    angles = positions.astype(jnp.float32)[:, None] * frequency[None, :]
    cos_part = jnp.concatenate([jnp.cos(angles), jnp.cos(angles)], axis=1)[:, None, :]
    sin_part = jnp.concatenate([jnp.sin(angles), jnp.sin(angles)], axis=1)[:, None, :]
    low_half = per_head[..., :half_size]
    high_half = per_head[..., half_size:]
    turned = jnp.concatenate([-high_half, low_half], axis=-1)
    return (per_head * cos_part + turned * sin_part).reshape(states.shape)

def reference(tokens, norm_gain, kv_weight, adapter_down, adapter_up, token_adapters, adapter_slot, request_lengths):
    widened = tokens.astype(jnp.float32)
    squares = lax.optimization_barrier(jnp.sum(widened * widened, axis=1))
    normed = (widened * lax.rsqrt(squares / D + epsilon)[:, None] * norm_gain[None, :]).astype(jnp.bfloat16)
    base_part = jnp.dot(normed, kv_weight.reshape(D, 2 * KV), preferred_element_type=jnp.float32).reshape(TOKENS, 2, KV)
    down_float = adapter_down.astype(jnp.float32)
    up_float = adapter_up.astype(jnp.float32)

    def block_delta(block_args):
        block_rows, block_ids = block_args
        targets = place_rows(block_ids, adapter_slot, TOKENS_PER_ADAPT)
        buffer = jnp.zeros((ADAPTER_COUNT * TOKENS_PER_ADAPT, D), jnp.bfloat16).at[targets].set(block_rows)
        buffer = buffer.reshape(ADAPTER_COUNT, TOKENS_PER_ADAPT, D)
        down_projected = jnp.einsum('acd,adr->acr', buffer.astype(jnp.float32), down_float)
        rank_activation = (down_projected * adapter_scale).astype(jnp.bfloat16).reshape(ADAPTER_COUNT, TOKENS_PER_ADAPT, 2, ADAPTER_RANK)
        update_rows = jnp.einsum('acjr,ajrk->acjk', rank_activation.astype(jnp.float32), up_float).astype(jnp.bfloat16)
        return update_rows.reshape(ADAPTER_COUNT * TOKENS_PER_ADAPT, 2, KV)[targets]
    delta_rows = lax.map(block_delta, (normed.reshape(N_STORE, TOK_DEV, D), token_adapters[:, 0].reshape(N_STORE, TOK_DEV)))
    delta_rows = delta_rows.reshape(TOKENS, 2, KV)
    combined = base_part + delta_rows.astype(jnp.float32)
    positions = positions_of(jnp.zeros((), jnp.int32), TOKENS, request_lengths)
    new_keys = rotate(combined[:, 0, :], positions).astype(jnp.bfloat16)
    new_values = combined[:, 1, :].astype(jnp.bfloat16)
    return (new_keys, new_values)
```

```python
import functools
import math

import jax
import jax.numpy as jnp
from jax import lax
from jax.experimental import pallas as pl
from jax.experimental.pallas import tpu as pltpu
from jax.sharding import PartitionSpec as P

D = 8192
HEAD = 128
ADAPTER_RANK = 64


epsilon = 1e-05
adapter_scale = 2.0
rope_theta = 500000.0


def place_rows(adapter_ids, adapter_slot, capacity):
    catalog = jnp.arange(adapter_slot.shape[0], dtype=jnp.int32)
    slot_rows = jnp.sum(
        jnp.where(adapter_ids[:, None] == catalog[None, :], adapter_slot[None, :], 0), axis=1
    )
    row_order = jnp.arange(adapter_ids.shape[0], dtype=jnp.int32)
    same_earlier = (adapter_ids[:, None] == adapter_ids[None, :]) & (
        row_order[None, :] < row_order[:, None]
    )
    rank_rows = jnp.sum(same_earlier.astype(jnp.int32), axis=1)
    return slot_rows * capacity + rank_rows


def positions_of(first_row, row_count, lengths):
    global_rows = first_row + jnp.arange(row_count, dtype=jnp.int32)
    request_ends = jnp.cumsum(lengths)
    preceding = jnp.sum(
        jnp.where(request_ends[None, :] <= global_rows[:, None], lengths[None, :], 0), axis=1
    )
    return global_rows - preceding


def rotate(states, positions):
    per_head = states.reshape(states.shape[0], -1, HEAD)
    half_size = HEAD // 2
    frequency = jnp.exp(
        jnp.arange(half_size, dtype=jnp.float32) * (-2.0 * math.log(rope_theta) / HEAD)
    )
    angles = positions.astype(jnp.float32)[:, None] * frequency[None, :]
    cos_part = jnp.concatenate([jnp.cos(angles), jnp.cos(angles)], axis=1)[:, None, :]
    sin_part = jnp.concatenate([jnp.sin(angles), jnp.sin(angles)], axis=1)[:, None, :]
    low_half = per_head[..., :half_size]
    high_half = per_head[..., half_size:]
    turned = jnp.concatenate([-high_half, low_half], axis=-1)
    return (per_head * cos_part + turned * sin_part).reshape(states.shape)


MESH = pl.DeviceIdType.MESH


HALVES = 2


def fused_kernel(
    stores,
    tensors,
    cap,
    gain,
    ids,
    slots,
    lengths,
    tok_hbm,
    up_hbm,
    w_hbm,
    down_hbm,
    out,
    trow,
    tcol,
    cos_t,
    sin_t,
    scale_t,
    g,
    w3,
    w,
    down,
    up,
    own,
    snd,
    tin,
    sq_out,
    sq_in,
    acc,
    base_out,
    base_in,
    low_out,
    low_in,
    ret,
    ret_y,
    ret_t,
    tl_sem,
    w_sem,
    ld_sem,
    lu_sem,
    sq_ss,
    sq_rs,
    y_ss,
    y_rs,
    t_ss,
    t_rs,
    dn_ss,
    dn_fs,
    dn_rs,
    up_ss,
    up_rs,
    base_ss,
    base_rs,
    low_ss,
    low_rs,
    ret_ss,
    rt_ss,
    ret_rs,
):
    rows, width = tok_hbm.shape
    per = down_hbm.shape[0]
    depth = stores // 2
    col = depth * per
    moved = per + 1
    kv_local = up.shape[4]
    kv_whole = kv_local * tensors
    half_rows = width // HALVES
    me_s = lax.axis_index("store")
    me_t = lax.axis_index("tensor")
    z = me_s // 2
    y = me_s % 2
    low_side = z < 2
    is_mid = (z == 1) | (z == 2)
    is_end = (z == 0) | (z == 3)
    across = 3 - z
    inner = jnp.where(low_side, 1, 2)
    outer = jnp.where(low_side, 0, 3)
    z_next = jnp.where(is_mid, across, inner)
    first = jnp.where(is_mid, per, 0)

    def remote(src, dst, ss, rs, store, tensor):
        return pltpu.make_async_remote_copy(
            src_ref=src, dst_ref=dst, send_sem=ss, recv_sem=rs,
            device_id={"store": store, "tensor": tensor}, device_id_type=MESH,
        )

    def to_tensor(step):
        return (me_t + step) % tensors

    mate = me_t // 2 * 2 + 1 - me_t % 2
    far = (me_t + 2) % tensors
    far_mate = (mate + 2) % tensors
    beside = z * 2 + 1 - y

    def part_of(h):
        return pl.ds(h * half_rows, half_rows)

    tile = 128
    tok_loads = [
        pltpu.make_async_copy(
            tok_hbm.at[pl.ds(i * tile, tile)], g.at[pl.ds(i * tile, tile)], tl_sem.at[i]
        )
        for i in range(rows // tile)
    ]
    for load in tok_loads:
        load.start()
    wt = w3.shape[1]
    w_loads = [
        pltpu.make_async_copy(w_hbm.at[pl.ds(i * wt, wt)], w3.at[i % 2], w_sem.at[i % 2])
        for i in range(width // wt)
    ]
    own_loads = [
        pltpu.make_async_copy(down_hbm.at[l], down.at[first + l], ld_sem.at[l]) for l in range(per)
    ]
    up_load = pltpu.make_async_copy(up_hbm, up.at[first // per], lu_sem.at[0])

    barrier = pltpu.get_barrier_semaphore()
    for step in range(1, stores):
        pl.semaphore_signal(
            barrier, inc=1, device_id={"store": (me_s + step) % stores}, device_id_type=MESH
        )
    for step in range(1, tensors):
        pl.semaphore_signal(
            barrier, inc=1, device_id={"tensor": (me_t + step) % tensors}, device_id_type=MESH
        )
    w_loads[0].start()
    w_loads[1].start()
    for load in own_loads:
        load.start()
    up_load.start()
    pl.semaphore_wait(barrier, stores + tensors - 2)

    def own_send(l, h):
        k = jnp.where(is_mid, 2 * per + l, l)
        return remote(
            down_hbm.at[l, part_of(h)], down.at[k, part_of(h)], dn_ss.at[l, h], dn_rs.at[k, h],
            z_next * 2 + y, me_t,
        )

    def up_send():
        q = jnp.where(is_mid, 2, 0)
        return remote(up_hbm, up.at[q], up_ss.at[0], up_rs.at[q], z_next * 2 + y, me_t)

    def forward(k, h):
        if k < per:
            to, at = across, k + 3 * per
        else:
            to, at = outer, k
        return remote(
            down.at[k, part_of(h)], down.at[at, part_of(h)], dn_fs.at[k, h], dn_rs.at[at, h],
            to * 2 + y, me_t,
        )

    def up_forward(q):
        to, at = (across, 3) if q == 0 else (outer, q)
        return remote(up.at[q], up.at[at], up_ss.at[1 + q], up_rs.at[at], to * 2 + y, me_t)

    def arrived(k, h):
        return remote(
            down.at[k, part_of(h)], down.at[k, part_of(h)], dn_fs.at[k, h], dn_rs.at[k, h],
            z_next * 2 + y, me_t,
        )

    def up_arrived(q):
        return remote(up.at[q], up.at[q], up_ss.at[1 + q], up_rs.at[q], z_next * 2 + y, me_t)

    forwarded = [k for k in range(col) if k < per or k > 2 * per]

    @pl.when(is_mid)
    def _():
        up_send().start()
        for l in range(1, per):
            for h in range(HALVES):
                own_send(l, h).start()

    @pl.when(is_end)
    def _():
        up_send().start()
        for h in range(HALVES):
            own_send(0, h).start()

    adapters = slots.shape[0]
    named = jnp.where(
        lax.broadcasted_iota(jnp.int32, (adapters, rows), 0) == ids[...], 1.0, 0.0
    )
    earlier = jnp.where(
        lax.broadcasted_iota(jnp.int32, (rows, rows), 0)
        < lax.broadcasted_iota(jnp.int32, (rows, rows), 1),
        1.0,
        0.0,
    ).astype(jnp.bfloat16)
    counts = jnp.dot(named.astype(jnp.bfloat16), earlier, preferred_element_type=jnp.float32)
    rank = jnp.sum(named * counts, axis=0, keepdims=True).astype(jnp.int32)
    slot = jnp.zeros((1, rows), jnp.int32)
    for a in range(adapters):
        slot = jnp.where(ids[...] == a, slots[a], slot)
    owner = slot // per
    plane = owner // 2
    place = jnp.where(low_side, plane, depth - 1 - plane) * per + slot % per
    other = jnp.where(owner % 2 == y, 0, col)
    trow[...] = (other + place) * cap + rank

    def scale(i, _):
        at = pl.ds(pl.multiple_of(i * tile, tile), tile)
        pltpu.make_async_copy(tok_hbm.at[at], g.at[at], tl_sem.at[i]).wait()
        x = g[at, :].astype(jnp.float32)
        g[at, :] = (x * gain[...]).astype(jnp.bfloat16)
        total = x[:, 0:128] * x[:, 0:128]
        for lane in range(1, width // 128):
            part = x[:, lane * 128 : (lane + 1) * 128]
            total = total + part * part
        sq_out[:, at] = jnp.broadcast_to(jnp.sum(total.T, axis=0, keepdims=True), (8, tile))
        return 0

    lax.fori_loop(0, rows // tile, scale, 0)

    sq_copies = [
        remote(sq_out, sq_in.at[m - 1], sq_ss.at[m - 1], sq_rs.at[m - 1], me_s, to_tensor(m))
        for m in range(1, tensors)
    ]
    for copy in sq_copies:
        copy.start()

    chunk = 512
    batch = col // 2

    def pick(group, store):
        places = lax.broadcasted_iota(jnp.int32, (batch * cap, rows), 0) + group * cap
        choose = jnp.where(places == trow[...], 1.0, 0.0).astype(jnp.bfloat16)

        def part(i, _):
            at = pl.ds(pl.multiple_of(i * chunk, chunk), chunk)
            r = jnp.dot(choose, g[:, at], preferred_element_type=jnp.float32)
            store(at, r.astype(jnp.bfloat16).reshape(batch, cap, chunk))
            return 0

        lax.fori_loop(0, width // chunk, part, 0)

    def y_copy(k):
        return remote(snd.at[k], own.at[k, 1], y_ss.at[k], y_rs.at[k], beside, me_t)

    def t_copy(j, cross):
        src = snd.at[per + j] if cross else own.at[per + j, 0]
        to = inner * 2 + (1 - y if cross else y)
        return remote(src, tin.at[j, cross], t_ss.at[j, cross], t_rs.at[j, cross], to, me_t)

    for b in range(2):
        def to_snd(at, r, b=b):
            snd[b * batch : (b + 1) * batch, :, at] = r

        pick(col + b * batch, to_snd)

    mid_order = [4, 5, 6, 7, 9, 0, 10, 11, 1, 12, 13, 2, 8, 3, 14, 15]
    end_order = [0, 1, 2, 3, 9, 10, 11, 12, 13, 14, 15]

    @pl.when(is_mid)
    def _():
        for k in mid_order:
            y_copy(k).start()

    @pl.when(is_end)
    def _():
        for j in (0, 1):
            t_copy(j, 1).start()
        for k in end_order[:4]:
            y_copy(k).start()
        for j in (2, 3):
            t_copy(j, 1).start()
        for k in end_order[4:8]:
            y_copy(k).start()
        t_copy(4, 1).start()
        for k in end_order[8:]:
            y_copy(k).start()

    for b in range(2):
        def to_own(at, r, b=b):
            own[b * batch : (b + 1) * batch, 0, :, at] = r

        pick(b * batch, to_own)

    @pl.when(is_end)
    def _():
        t_copy(0, 0).start()
        t_copy(1, 0).start()
        for h in range(HALVES):
            own_send(1, h).start()
        t_copy(2, 0).start()
        t_copy(3, 0).start()
        for l in (2, 3):
            for h in range(HALVES):
                own_send(l, h).start()
        t_copy(4, 0).start()

    def mid(body):
        pl.when(is_mid)(body)

    def pump(k):
        def body():
            for h in range(HALVES):
                arrived(k, h).wait_recv()
                if k in forwarded:
                    forward(k, h).start()

        mid(body)

    def pump_up(q):
        def body():
            up_arrived(q).wait_recv()
            up_forward(q).start()

        mid(body)

    pump_up(2)
    pump_up(0)
    pump(9)
    pump(0)

    dt = 128
    two = lax.broadcasted_iota(jnp.int32, (dt, 2 * dt), 1) - 2 * lax.broadcasted_iota(
        jnp.int32, (dt, 2 * dt), 0
    )
    every = [jnp.where(two == j, 1.0, 0.0).astype(jnp.bfloat16) for j in range(2)]
    for i in range(width // wt):
        w_loads[i].wait()

        def part_kinds(n, _, i=i):
            x = w3[i % 2, pl.ds(pl.multiple_of(n * dt, dt), dt)].reshape(2 * dt, kv_whole)
            at = pl.ds(pl.multiple_of(i * wt + n * dt, dt), dt)
            for j in range(2):
                w[at, j * kv_whole : (j + 1) * kv_whole] = jnp.dot(
                    every[j], x, preferred_element_type=jnp.float32
                ).astype(jnp.bfloat16)
            return 0

        lax.fori_loop(0, wt // dt, part_kinds, 0)
        if i + 2 < width // wt:
            w_loads[i + 2].start()

    mt = 256
    base_copies = [
        remote(base_out.at[n], base_in.at[n], base_ss.at[n], base_rs.at[n], me_s, to)
        for n, to in enumerate((mate, mate, far))
    ]

    def base(target, store):
        for j in range(2):
            cols = pl.ds(pl.multiple_of(j * kv_whole + target * kv_local, kv_local), kv_local)

            def part(i, _, j=j, cols=cols):
                at = pl.ds(pl.multiple_of(i * mt, mt), mt)
                r = jnp.dot(g[at, :], w[:, cols], preferred_element_type=jnp.float32)
                store(at, slice(j * kv_local, (j + 1) * kv_local), r)
                return 0

            lax.fori_loop(0, rows // mt, part, 0)

    def base_to(n):
        def store(at, cols, r):
            base_out[n, at, cols] = r.astype(jnp.bfloat16)

        return store

    def base_sum(at, cols, r):
        base_out[2, at, cols] = (r + base_in[0, at, cols].astype(jnp.float32)).astype(jnp.bfloat16)

    def base_own(at, cols, r):
        acc[at, cols] = r + base_in[1, at, cols].astype(jnp.float32)

    base(far_mate, base_to(0))
    base_copies[0].start()
    base(mate, base_to(1))
    base_copies[1].start()
    pump(10)
    base_copies[0].wait_recv()
    base(far, base_sum)
    base_copies[2].start()
    base_copies[1].wait_recv()
    base(me_t, base_own)
    pump(11)

    half = HEAD // 2
    lane = lax.broadcasted_iota(jnp.int32, (1, HEAD), 1)
    frequency = jnp.exp(
        (lane % half).astype(jnp.float32) * (-2.0 * math.log(rope_theta) / HEAD)
    )
    sign = jnp.where(lane < half, -1.0, 1.0)

    def tables(i, _):
        at = pl.ds(pl.multiple_of(i * tile, tile), tile)
        row = lax.broadcasted_iota(jnp.int32, (tile, HEAD), 0) + (me_s * rows + i * tile)
        position = row
        end = 0
        for r in range(lengths.shape[0]):
            end = end + lengths[r]
            position = jnp.where(row >= end, row - end, position)
        angles = position.astype(jnp.float32) * frequency
        cos_t[at, :] = jnp.cos(angles)
        sin_t[at, :] = jnp.sin(angles) * sign
        tcol[at, :] = jnp.broadcast_to(trow[:, at], (tile, tile)).T
        return 0

    def low_copy(n, m):
        return remote(
            low_out.at[n], low_in.at[m - 1, n], low_ss.at[n, m - 1], low_rs.at[n, m - 1],
            me_s, to_tensor(m),
        )

    def lower_rows(n, k, x):
        low_out[n] = jnp.dot(x, down[k], preferred_element_type=jnp.float32)
        for m in range(1, tensors):
            low_copy(n, m).start()

    def lower(k):
        y_copy(k).wait_recv()
        lower_rows(k, k, own[k].reshape(2 * cap, width))

    def lower_moved(j):
        t_copy(j, 0).wait_recv()
        t_copy(j, 1).wait_recv()
        lower_rows(col + j, per + j, tin[j].reshape(2 * cap, width))

    def raised(n, k):
        total = low_out[n]
        for m in range(1, tensors):
            low_copy(n, m).wait_recv()
            total = total + low_in[m - 1, n]
        middle = (total * adapter_scale).astype(jnp.bfloat16)
        return [
            jnp.dot(
                middle[:, j * ADAPTER_RANK : (j + 1) * ADAPTER_RANK],
                up[k // per, k % per, j],
                preferred_element_type=jnp.float32,
            ).astype(jnp.bfloat16)
            for j in range(2)
        ]

    def ret_copy(k):
        return remote(
            ret_y.at[k], ret.at[col + k], ret_ss.at[k], ret_rs.at[col + k], beside, me_t
        )

    def moved_copy(j, cross):
        at = per + j + (col if cross else 0)
        to = outer * 2 + (1 - y if cross else y)
        return remote(ret_t.at[j, cross], ret.at[at], rt_ss.at[j, cross], ret_rs.at[at], to, me_t)

    def raise_back(k):
        for j, d in enumerate(raised(k, k)):
            cols = slice(j * kv_local, (j + 1) * kv_local)
            ret[k, :, cols] = d[:cap]
            ret_y[k, :, cols] = d[cap:]
        ret_copy(k).start()

    def raise_moved(n):
        for j, d in enumerate(raised(col + n, per + n)):
            cols = slice(j * kv_local, (j + 1) * kv_local)
            ret_t[n, 0, :, cols] = d[:cap]
            ret_t[n, 1, :, cols] = d[cap:]
        moved_copy(n, 0).start()
        moved_copy(n, 1).start()

    def lower_far(k):
        @pl.when(is_end)
        def _():
            for h in range(HALVES):
                arrived(k, h).wait_recv()

        lower(k)

    def give(lo, hi):
        count = (hi - lo) * cap

        def part(i, _):
            at = pl.ds(pl.multiple_of(i * mt, mt), mt)
            lanes = lax.broadcasted_iota(jnp.int32, (mt, count), 1)
            total = acc[at, :]
            for start in (lo, col + lo):
                choose = jnp.where(lanes + start * cap == tcol[at, 0:1], 1.0, 0.0)
                total = total + jnp.dot(
                    choose.astype(jnp.bfloat16),
                    ret[start : start + hi - lo].reshape(count, 2 * kv_local),
                    preferred_element_type=jnp.float32,
                )
            acc[at, :] = total
            return 0

        lax.fori_loop(0, rows // mt, part, 0)

    def join(i, _):
        at = pl.ds(pl.multiple_of(i * tile, tile), tile)
        square = sq_out[0:1, at]
        for m in range(tensors - 1):
            square = square + sq_in[m, 0:1, at]
        scale_row = lax.rsqrt(square / (width * tensors) + epsilon)
        scale_t[at, :] = jnp.broadcast_to(scale_row, (tile, tile)).T
        acc[at, :] = acc[at, :] + base_in[2, at, :].astype(jnp.float32)
        return 0

    for load in own_loads:
        load.wait()
    up_load.wait()
    for l in range(per):
        lower(first + l)
    lax.fori_loop(0, rows // tile, tables, 0)
    lower_far(9)
    for l in range(per):
        raise_back(first + l)

    @pl.when(is_end)
    def _():
        up_arrived(2).wait_recv()

    mid(lambda: lower(0))
    lower_far(10)
    raise_back(9)
    mid(lambda: raise_back(0))
    lower_far(11)
    raise_back(10)

    @pl.when(is_mid)
    def _():
        up_arrived(3).wait_recv()
        up_forward(3).start()
        lower_moved(0)
        lower_moved(1)

    pump(1)

    @pl.when(is_mid)
    def _():
        for h in range(HALVES):
            own_send(0, h).start()
        lower(1)

    raise_back(11)

    @pl.when(is_mid)
    def _():
        raise_moved(0)
        raise_moved(1)

    for copy in sq_copies:
        copy.wait_recv()
    base_copies[2].wait_recv()
    lax.fori_loop(0, rows // tile, join, 0)

    @pl.when(is_end)
    def _():
        up_arrived(3).wait_recv()

    pump(12)
    lower_far(12)
    mid(lambda: raise_back(1))

    @pl.when(is_mid)
    def _():
        lower_moved(2)
        lower_moved(3)

    raise_back(12)

    @pl.when(is_mid)
    def _():
        raise_moved(2)
        raise_moved(3)

    pump(13)
    lower_far(13)
    pump(2)
    mid(lambda: lower(2))
    raise_back(13)
    mid(lambda: raise_back(2))
    pump(8)
    mid(lambda: lower(8))
    pump(3)

    @pl.when(is_mid)
    def _():
        lower(3)
        raise_back(8)

    pump(14)
    lower_far(14)

    @pl.when(is_mid)
    def _():
        raise_back(3)
        lower_moved(4)

    raise_back(14)
    mid(lambda: raise_moved(4))

    late = 14
    for k in end_order:
        if k < late:
            ret_copy(k).wait_recv()

    @pl.when(is_mid)
    def _():
        for k in mid_order:
            if k not in end_order:
                ret_copy(k).wait_recv()

    @pl.when(is_end)
    def _():
        for j in range(moved):
            for cross in range(2):
                moved_copy(j, cross).wait_recv()

    give(0, late)
    pump(15)
    lower_far(15)
    raise_back(15)
    for k in range(late, col):
        ret_copy(k).wait_recv()
    give(late, col)

    def finish(i, _):
        at = pl.ds(pl.multiple_of(i * tile, tile), tile)
        total = acc[at, :] * scale_t[at, 0:1]
        c = cos_t[at, :]
        s = sin_t[at, :]
        for head in range(kv_local // HEAD):
            x = total[:, head * HEAD : (head + 1) * HEAD]
            r = x * c + pltpu.roll(x, HEAD // 2, 1) * s
            out[at, head * HEAD : (head + 1) * HEAD] = r.astype(jnp.bfloat16)
        out[at, kv_local:] = total[:, kv_local:].astype(jnp.bfloat16)
        return 0

    lax.fori_loop(0, rows // tile, finish, 0)

    for copy in sq_copies + base_copies:
        copy.wait_send()
    up_send().wait_send()
    for l in range(per):
        for h in range(HALVES):
            own_send(l, h).wait_send()
    for i, k in enumerate(end_order):
        k = first + i if i < per else k
        y_copy(k).wait_send()
        ret_copy(k).wait_send()
        for m in range(1, tensors):
            low_copy(k, m).wait_send()

    @pl.when(is_mid)
    def _():
        for k in forwarded:
            for h in range(HALVES):
                forward(k, h).wait_send()
        for q in (0, 2, 3):
            up_forward(q).wait_send()
        for k in (0, 1, 2, 3, 8):
            y_copy(k).wait_send()
            ret_copy(k).wait_send()
            for m in range(1, tensors):
                low_copy(k, m).wait_send()
        for j in range(moved):
            for m in range(1, tensors):
                low_copy(col + j, m).wait_send()
            for cross in range(2):
                moved_copy(j, cross).wait_send()

    @pl.when(is_end)
    def _():
        for j in range(moved):
            for cross in range(2):
                t_copy(j, cross).wait_send()


def fused(
    tokens,
    norm_gain,
    kv_weight,
    adapter_down,
    adapter_up,
    token_adapters,
    adapter_slot,
    request_lengths,
):
    rows, width = tokens.shape
    capacity = max(2, 5 * rows // (4 * adapter_slot.shape[0]))
    cap = -(-capacity // 16) * 16
    stores = lax.axis_size("store")
    tensors = lax.axis_size("tensor")
    per, _, _, kv_local = adapter_up.shape
    depth = stores // 2
    col = depth * per
    moved = per + 1
    ranks = adapter_down.shape[2]
    vmem = pl.BlockSpec(memory_space=pltpu.VMEM)
    smem = pl.BlockSpec(memory_space=pltpu.SMEM)
    hbm = pl.BlockSpec(memory_space=pl.ANY)
    f32, bf16 = jnp.float32, jnp.bfloat16
    dma = pltpu.SemaphoreType.DMA
    both = pl.pallas_call(
        functools.partial(fused_kernel, stores, tensors, cap),
        out_shape=jax.ShapeDtypeStruct((rows, 2 * kv_local), bf16),
        in_specs=[vmem] * 2 + [smem] * 2 + [hbm] * 4,
        out_specs=vmem,
        scratch_shapes=[
            pltpu.VMEM((1, rows), jnp.int32),
            pltpu.VMEM((rows, 128), jnp.int32),
            pltpu.VMEM((rows, HEAD), f32),
            pltpu.VMEM((rows, HEAD), f32),
            pltpu.VMEM((rows, 128), f32),
            pltpu.VMEM((rows, width), bf16),
            pltpu.VMEM((2, 256, 2, kv_local * tensors), bf16),
            pltpu.VMEM((width, 2 * kv_local * tensors), bf16),
            pltpu.VMEM((col, width, ranks), bf16),
            pltpu.VMEM((depth, per, 2, ADAPTER_RANK, kv_local), bf16),
            pltpu.VMEM((col, 2, cap, width), bf16),
            pltpu.VMEM((col, cap, width), bf16),
            pltpu.VMEM((moved, 2, cap, width), bf16),
            pltpu.VMEM((8, rows), f32),
            pltpu.VMEM((tensors - 1, 8, rows), f32),
            pltpu.VMEM((rows, 2 * kv_local), f32),
            pltpu.VMEM((3, rows, 2 * kv_local), bf16),
            pltpu.VMEM((3, rows, 2 * kv_local), bf16),
            pltpu.VMEM((col + moved, 2 * cap, ranks), f32),
            pltpu.VMEM((tensors - 1, col + moved, 2 * cap, ranks), f32),
            pltpu.VMEM((2 * col, cap, 2 * kv_local), bf16),
            pltpu.VMEM((col, cap, 2 * kv_local), bf16),
            pltpu.VMEM((moved, 2, cap, 2 * kv_local), bf16),
            dma((rows // 128,)),
            dma((2,)),
            dma((per,)),
            dma((1,)),
            dma((tensors - 1,)),
            dma((tensors - 1,)),
            dma((col,)),
            dma((col,)),
            dma((moved, 2)),
            dma((moved, 2)),
            dma((per, HALVES)),
            dma((col, HALVES)),
            dma((col, HALVES)),
            dma((1 + depth,)),
            dma((depth,)),
            dma((3,)),
            dma((3,)),
            dma((col + moved, tensors - 1)),
            dma((col + moved, tensors - 1)),
            dma((col,)),
            dma((moved, 2)),
            dma((2 * col,)),
        ],
        compiler_params=pltpu.CompilerParams(
            collective_id=0, has_side_effects=True, vmem_limit_bytes=63 * 1024 * 1024
        ),
    )(
        norm_gain[None, :],
        token_adapters.reshape(1, rows),
        adapter_slot,
        request_lengths,
        tokens,
        adapter_up,
        kv_weight,
        adapter_down,
    )
    return both[:, :kv_local], both[:, kv_local:]


def local(
    tokens,
    norm_gain,
    kv_weight,
    adapter_down,
    adapter_up,
    token_adapters,
    adapter_slot,
    request_lengths,
):
    row_count = tokens.shape[0]
    local_width = tokens.shape[1]
    adapter_total = adapter_slot.shape[0]
    capacity = max(2, 5 * row_count // (4 * adapter_total))
    store_size = lax.axis_size("store")
    per_owner = adapter_down.shape[0]
    kv_local = adapter_up.shape[3]
    widened = tokens.astype(jnp.float32)
    squares = lax.psum(jnp.sum(widened * widened, axis=1), "tensor")
    normed = (widened * lax.rsqrt(squares / D + epsilon)[:, None] * norm_gain[None, :]).astype(
        jnp.bfloat16
    )
    targets = place_rows(token_adapters[:, 0], adapter_slot, capacity)
    send_rows = (
        jnp.zeros((adapter_total * capacity, local_width), jnp.bfloat16).at[targets].set(normed)
    )
    send_rows = send_rows.reshape(store_size, per_owner, capacity, local_width)
    down_projected = jnp.einsum(
        "slcd,ldr->slcr",
        lax.all_to_all(send_rows, "store", split_axis=0, concat_axis=0, tiled=True),
        adapter_down,
        preferred_element_type=jnp.float32,
    )
    rank_total_sum = lax.psum(down_projected, "tensor")
    rank_activation = (rank_total_sum * adapter_scale).astype(jnp.bfloat16)
    split_rank = rank_activation.reshape(rank_activation.shape[:3] + (2, ADAPTER_RANK))
    update_rows = jnp.einsum(
        "slcjr,ljrk->slcjk", split_rank, adapter_up, preferred_element_type=jnp.float32
    )
    back_rows = update_rows.astype(jnp.bfloat16).reshape(
        rank_activation.shape[:3] + (2 * kv_local,)
    )
    returned = lax.all_to_all(back_rows, "store", split_axis=0, concat_axis=0, tiled=True)
    delta_rows = returned.reshape(adapter_total * capacity, 2, kv_local)[targets]
    partial_value = jnp.einsum("td,djk->tjk", normed, kv_weight, preferred_element_type=jnp.float32)
    base_part = lax.psum_scatter(partial_value, "tensor", scatter_dimension=2, tiled=True)
    combined = base_part + delta_rows.astype(jnp.float32)
    positions = positions_of(lax.axis_index("store") * row_count, row_count, request_lengths)
    new_keys = rotate(combined[:, 0, :], positions).astype(jnp.bfloat16)
    new_values = combined[:, 1, :].astype(jnp.bfloat16)
    return (new_keys, new_values)


def solution(mesh):
    small = mesh.shape["store"] == 8 and mesh.shape["tensor"] == 4
    return jax.shard_map(
        fused if small else local,
        mesh=mesh,
        in_specs=(
            P("store", "tensor"),
            P("tensor"),
            P("tensor", None, None),
            P("store", "tensor", None),
            P("store", None, None, "tensor"),
            P("store", None),
            P(),
            P(),
        ),
        out_specs=(P("store", "tensor"), P("store", "tensor")),
        check_vma=False,
    )
```

```python
import functools
import math

import jax
import jax.numpy as jnp
from jax import lax
from jax.experimental import pallas as pl
from jax.experimental.pallas import tpu as pltpu
from jax.sharding import PartitionSpec as P

D = 8192
HEAD = 128
ADAPTER_RANK = 64


epsilon = 1e-05
adapter_scale = 2.0
rope_theta = 500000.0


def place_rows(adapter_ids, adapter_slot, capacity):
    catalog = jnp.arange(adapter_slot.shape[0], dtype=jnp.int32)
    slot_rows = jnp.sum(
        jnp.where(adapter_ids[:, None] == catalog[None, :], adapter_slot[None, :], 0), axis=1
    )
    row_order = jnp.arange(adapter_ids.shape[0], dtype=jnp.int32)
    same_earlier = (adapter_ids[:, None] == adapter_ids[None, :]) & (
        row_order[None, :] < row_order[:, None]
    )
    rank_rows = jnp.sum(same_earlier.astype(jnp.int32), axis=1)
    return slot_rows * capacity + rank_rows


def positions_of(first_row, row_count, lengths):
    global_rows = first_row + jnp.arange(row_count, dtype=jnp.int32)
    request_ends = jnp.cumsum(lengths)
    preceding = jnp.sum(
        jnp.where(request_ends[None, :] <= global_rows[:, None], lengths[None, :], 0), axis=1
    )
    return global_rows - preceding


def rotate(states, positions):
    per_head = states.reshape(states.shape[0], -1, HEAD)
    half_size = HEAD // 2
    frequency = jnp.exp(
        jnp.arange(half_size, dtype=jnp.float32) * (-2.0 * math.log(rope_theta) / HEAD)
    )
    angles = positions.astype(jnp.float32)[:, None] * frequency[None, :]
    cos_part = jnp.concatenate([jnp.cos(angles), jnp.cos(angles)], axis=1)[:, None, :]
    sin_part = jnp.concatenate([jnp.sin(angles), jnp.sin(angles)], axis=1)[:, None, :]
    low_half = per_head[..., :half_size]
    high_half = per_head[..., half_size:]
    turned = jnp.concatenate([-high_half, low_half], axis=-1)
    return (per_head * cos_part + turned * sin_part).reshape(states.shape)


MESH = pl.DeviceIdType.MESH


HALVES = 2


def fused_kernel(
    stores,
    tensors,
    cap,
    gain,
    ids,
    slots,
    lengths,
    tok_hbm,
    up_hbm,
    w_hbm,
    down_hbm,
    out,
    trow,
    tcol,
    cos_t,
    sin_t,
    scale_t,
    g,
    w3,
    w,
    down,
    up,
    own,
    snd,
    tin,
    sq_out,
    sq_in,
    acc,
    base_out,
    base_in,
    low_own,
    low_out,
    low_in,
    ret,
    ret_y,
    ret_t,
    tl_sem,
    w_sem,
    ld_sem,
    lu_sem,
    sq_ss,
    sq_rs,
    y_ss,
    y_rs,
    t_ss,
    t_rs,
    dn_ss,
    dn_fs,
    dn_rs,
    up_ss,
    up_rs,
    base_ss,
    base_rs,
    low_ss,
    low_rs,
    ret_ss,
    rt_ss,
    ret_rs,
):
    rows, width = tok_hbm.shape
    per = down_hbm.shape[0]
    depth = stores // 2
    col = depth * per
    moved = per + 2
    kv_local = up.shape[4]
    kv_whole = kv_local * tensors
    half_rows = width // HALVES
    me_s = lax.axis_index("store")
    me_t = lax.axis_index("tensor")
    z = me_s // 2
    y = me_s % 2
    low_side = z < 2
    is_mid = (z == 1) | (z == 2)
    is_end = (z == 0) | (z == 3)
    across = 3 - z
    inner = jnp.where(low_side, 1, 2)
    outer = jnp.where(low_side, 0, 3)
    z_next = jnp.where(is_mid, across, inner)
    first = jnp.where(is_mid, per, 0)

    def remote(src, dst, ss, rs, store, tensor):
        return pltpu.make_async_remote_copy(
            src_ref=src, dst_ref=dst, send_sem=ss, recv_sem=rs,
            device_id={"store": store, "tensor": tensor}, device_id_type=MESH,
        )

    def to_tensor(step):
        return (me_t + step) % tensors

    mate = me_t // 2 * 2 + 1 - me_t % 2
    far = (me_t + 2) % tensors
    far_mate = (mate + 2) % tensors
    beside = z * 2 + 1 - y

    def part_of(h):
        return pl.ds(h * half_rows, half_rows)

    tile = 128
    tok_loads = [
        pltpu.make_async_copy(
            tok_hbm.at[pl.ds(i * tile, tile)], g.at[pl.ds(i * tile, tile)], tl_sem.at[i]
        )
        for i in range(rows // tile)
    ]
    for load in tok_loads:
        load.start()
    wt = w3.shape[1]
    w_loads = [
        pltpu.make_async_copy(w_hbm.at[pl.ds(i * wt, wt)], w3.at[i % 2], w_sem.at[i % 2])
        for i in range(width // wt)
    ]
    own_loads = [
        pltpu.make_async_copy(down_hbm.at[l], down.at[first + l], ld_sem.at[l]) for l in range(per)
    ]
    up_load = pltpu.make_async_copy(up_hbm, up.at[first // per], lu_sem.at[0])

    barrier = pltpu.get_barrier_semaphore()
    for step in range(1, stores):
        pl.semaphore_signal(
            barrier, inc=1, device_id={"store": (me_s + step) % stores}, device_id_type=MESH
        )
    for step in range(1, tensors):
        pl.semaphore_signal(
            barrier, inc=1, device_id={"tensor": (me_t + step) % tensors}, device_id_type=MESH
        )
    w_loads[0].start()
    w_loads[1].start()
    for load in own_loads:
        load.start()
    up_load.start()
    pl.semaphore_wait(barrier, stores + tensors - 2)

    def own_send(l, h):
        k = jnp.where(is_mid, 2 * per + l, l)
        return remote(
            down_hbm.at[l, part_of(h)], down.at[k, part_of(h)], dn_ss.at[l, h], dn_rs.at[k, h],
            z_next * 2 + y, me_t,
        )

    def up_send():
        q = jnp.where(is_mid, 2, 0)
        return remote(up_hbm, up.at[q], up_ss.at[0], up_rs.at[q], z_next * 2 + y, me_t)

    def forward(k, h):
        if k < per:
            to, at = across, k + 3 * per
        else:
            to, at = outer, k
        return remote(
            down.at[k, part_of(h)], down.at[at, part_of(h)], dn_fs.at[k, h], dn_rs.at[at, h],
            to * 2 + y, me_t,
        )

    def up_forward(q):
        to, at = (across, 3) if q == 0 else (outer, q)
        return remote(up.at[q], up.at[at], up_ss.at[1 + q], up_rs.at[at], to * 2 + y, me_t)

    def arrived(k, h):
        return remote(
            down.at[k, part_of(h)], down.at[k, part_of(h)], dn_fs.at[k, h], dn_rs.at[k, h],
            z_next * 2 + y, me_t,
        )

    def up_arrived(q):
        return remote(up.at[q], up.at[q], up_ss.at[1 + q], up_rs.at[q], z_next * 2 + y, me_t)

    forwarded = [k for k in range(col) if not per <= k < per + moved]

    @pl.when(is_mid)
    def _():
        up_send().start()
        for l in (2, 3):
            for h in range(HALVES):
                own_send(l, h).start()

    @pl.when(is_end)
    def _():
        up_send().start()
        for h in range(HALVES):
            own_send(0, h).start()

    adapters = slots.shape[0]
    named = jnp.where(
        lax.broadcasted_iota(jnp.int32, (adapters, rows), 0) == ids[...], 1.0, 0.0
    )
    earlier = jnp.where(
        lax.broadcasted_iota(jnp.int32, (rows, rows), 0)
        < lax.broadcasted_iota(jnp.int32, (rows, rows), 1),
        1.0,
        0.0,
    ).astype(jnp.bfloat16)
    counts = jnp.dot(named.astype(jnp.bfloat16), earlier, preferred_element_type=jnp.float32)
    rank = jnp.sum(named * counts, axis=0, keepdims=True).astype(jnp.int32)
    slot = jnp.zeros((1, rows), jnp.int32)
    for a in range(adapters):
        slot = jnp.where(ids[...] == a, slots[a], slot)
    owner = slot // per
    plane = owner // 2
    place = jnp.where(low_side, plane, depth - 1 - plane) * per + slot % per
    other = jnp.where(owner % 2 == y, 0, col)
    trow[...] = (other + place) * cap + rank

    def scale(i, _):
        at = pl.ds(pl.multiple_of(i * tile, tile), tile)
        pltpu.make_async_copy(tok_hbm.at[at], g.at[at], tl_sem.at[i]).wait()
        x = g[at, :].astype(jnp.float32)
        g[at, :] = (x * gain[...]).astype(jnp.bfloat16)
        total = x[:, 0:128] * x[:, 0:128]
        for lane in range(1, width // 128):
            part = x[:, lane * 128 : (lane + 1) * 128]
            total = total + part * part
        sq_out[:, at] = jnp.broadcast_to(jnp.sum(total.T, axis=0, keepdims=True), (8, tile))
        return 0

    lax.fori_loop(0, rows // tile, scale, 0)

    sq_copies = [
        remote(sq_out, sq_in.at[m - 1], sq_ss.at[m - 1], sq_rs.at[m - 1], me_s, to_tensor(m))
        for m in range(1, tensors)
    ]
    for copy in sq_copies:
        copy.start()

    chunk = 512
    batch = col // 2

    def pick(group, store):
        places = lax.broadcasted_iota(jnp.int32, (batch * cap, rows), 0) + group * cap
        choose = jnp.where(places == trow[...], 1.0, 0.0).astype(jnp.bfloat16)

        def part(i, _):
            at = pl.ds(pl.multiple_of(i * chunk, chunk), chunk)
            r = jnp.dot(choose, g[:, at], preferred_element_type=jnp.float32)
            store(at, r.astype(jnp.bfloat16).reshape(batch, cap, chunk))
            return 0

        lax.fori_loop(0, width // chunk, part, 0)

    def y_copy(k):
        return remote(snd.at[k], own.at[k, 1], y_ss.at[k], y_rs.at[k], beside, me_t)

    def t_copy(j):
        return remote(
            own.at[per + j], tin.at[j], t_ss.at[j], t_rs.at[j], inner * 2 + y, me_t
        )

    for b in range(2):
        def to_snd(at, r, b=b):
            snd[b * batch : (b + 1) * batch, :, at] = r

        pick(col + b * batch, to_snd)

    mid_order = [4, 5, 6, 7, 10, 0, 11, 1, 12, 13, 2, 14, 3, 9, 15, 8]
    end_order = [4, 0, 1, 2, 3, 5, 6, 10, 7, 11, 9, 8, 12, 13, 14, 15]

    @pl.when(is_mid)
    def _():
        for k in mid_order:
            y_copy(k).start()

    @pl.when(is_end)
    def _():
        for k in end_order:
            y_copy(k).start()

    for b in range(2):
        def to_own(at, r, b=b):
            own[b * batch : (b + 1) * batch, 0, :, at] = r

        pick(b * batch, to_own)

    def mid(body):
        pl.when(is_mid)(body)

    def pump(k):
        def body():
            for h in range(HALVES):
                arrived(k, h).wait_recv()
                if k in forwarded:
                    forward(k, h).start()

        mid(body)

    def pump_up(q):
        def body():
            up_arrived(q).wait_recv()
            up_forward(q).start()

        mid(body)

    def send_on(*moves):
        def body():
            for kind, n in moves:
                if kind == "own":
                    for h in range(HALVES):
                        own_send(n, h).start()
                else:
                    y_copy(per + n).wait_recv()
                    t_copy(n).start()

        pl.when(is_end)(body)

    send_on(("moved", 0), ("own", 1))
    pump_up(2)
    pump_up(0)

    dt = 128
    two = lax.broadcasted_iota(jnp.int32, (dt, 2 * dt), 1) - 2 * lax.broadcasted_iota(
        jnp.int32, (dt, 2 * dt), 0
    )
    every = [jnp.where(two == j, 1.0, 0.0).astype(jnp.bfloat16) for j in range(2)]
    for i in range(width // wt):
        w_loads[i].wait()

        def part_kinds(n, _, i=i):
            x = w3[i % 2, pl.ds(pl.multiple_of(n * dt, dt), dt)].reshape(2 * dt, kv_whole)
            at = pl.ds(pl.multiple_of(i * wt + n * dt, dt), dt)
            for j in range(2):
                w[at, j * kv_whole : (j + 1) * kv_whole] = jnp.dot(
                    every[j], x, preferred_element_type=jnp.float32
                ).astype(jnp.bfloat16)
            return 0

        lax.fori_loop(0, wt // dt, part_kinds, 0)
        if i + 2 < width // wt:
            w_loads[i + 2].start()

    mt = 256
    base_copies = [
        remote(base_out.at[n], base_in.at[n], base_ss.at[n], base_rs.at[n], me_s, to)
        for n, to in enumerate((mate, mate, far))
    ]

    def base(target, store):
        for j in range(2):
            cols = pl.ds(pl.multiple_of(j * kv_whole + target * kv_local, kv_local), kv_local)

            def part(i, _, j=j, cols=cols):
                at = pl.ds(pl.multiple_of(i * mt, mt), mt)
                r = jnp.dot(g[at, :], w[:, cols], preferred_element_type=jnp.float32)
                store(at, slice(j * kv_local, (j + 1) * kv_local), r)
                return 0

            lax.fori_loop(0, rows // mt, part, 0)

    def base_to(n):
        def store(at, cols, r):
            base_out[n, at, cols] = r.astype(jnp.bfloat16)

        return store

    def base_sum(at, cols, r):
        base_out[2, at, cols] = (r + base_in[0, at, cols].astype(jnp.float32)).astype(jnp.bfloat16)

    def base_own(at, cols, r):
        acc[at, cols] = r + base_in[1, at, cols].astype(jnp.float32)

    half = HEAD // 2
    lane = lax.broadcasted_iota(jnp.int32, (1, HEAD), 1)
    frequency = jnp.exp(
        (lane % half).astype(jnp.float32) * (-2.0 * math.log(rope_theta) / HEAD)
    )
    sign = jnp.where(lane < half, -1.0, 1.0)

    def tables(i, _):
        at = pl.ds(pl.multiple_of(i * tile, tile), tile)
        row = lax.broadcasted_iota(jnp.int32, (tile, HEAD), 0) + (me_s * rows + i * tile)
        position = row
        end = 0
        for r in range(lengths.shape[0]):
            end = end + lengths[r]
            position = jnp.where(row >= end, row - end, position)
        angles = position.astype(jnp.float32) * frequency
        cos_t[at, :] = jnp.cos(angles)
        sin_t[at, :] = jnp.sin(angles) * sign
        tcol[at, :] = jnp.broadcast_to(trow[:, at], (tile, tile)).T
        return 0

    def low_copy(n, m):
        return remote(
            low_out.at[n], low_in.at[m - 1, n], low_ss.at[n, m - 1], low_rs.at[n, m - 1],
            me_s, to_tensor(m),
        )

    def lower_rows(n, k, x):
        r = jnp.dot(x, down[k], preferred_element_type=jnp.float32)
        low_own[n] = r
        low_out[n] = r.astype(jnp.bfloat16)
        for m in range(1, tensors):
            low_copy(n, m).start()

    def lower(k):
        y_copy(k).wait_recv()
        lower_rows(k, k, own[k].reshape(2 * cap, width))

    def lower_moved(j):
        t_copy(j).wait_recv()
        lower_rows(col + j, per + j, tin[j].reshape(2 * cap, width))

    def raised(n, k):
        total = low_own[n]
        for m in range(1, tensors):
            low_copy(n, m).wait_recv()
            total = total + low_in[m - 1, n].astype(jnp.float32)
        middle = (total * adapter_scale).astype(jnp.bfloat16)
        return [
            jnp.dot(
                middle[:, j * ADAPTER_RANK : (j + 1) * ADAPTER_RANK],
                up[k // per, k % per, j],
                preferred_element_type=jnp.float32,
            ).astype(jnp.bfloat16)
            for j in range(2)
        ]

    def ret_copy(k):
        return remote(
            ret_y.at[k], ret.at[col + k], ret_ss.at[k], ret_rs.at[col + k], beside, me_t
        )

    def moved_copy(j, cross):
        at = per + j + (col if cross else 0)
        to = outer * 2 + (1 - y if cross else y)
        return remote(ret_t.at[j, cross], ret.at[at], rt_ss.at[j, cross], ret_rs.at[at], to, me_t)

    def raise_back(k):
        for j, d in enumerate(raised(k, k)):
            cols = slice(j * kv_local, (j + 1) * kv_local)
            ret[k, :, cols] = d[:cap]
            ret_y[k, :, cols] = d[cap:]
        ret_copy(k).start()

    def raise_moved(n):
        for j, d in enumerate(raised(col + n, per + n)):
            cols = slice(j * kv_local, (j + 1) * kv_local)
            ret_t[n, 0, :, cols] = d[:cap]
            ret_t[n, 1, :, cols] = d[cap:]
        moved_copy(n, 0).start()
        moved_copy(n, 1).start()

    def lower_far(k):
        @pl.when(is_end)
        def _():
            for h in range(HALVES):
                arrived(k, h).wait_recv()

        lower(k)

    def given(at, total, spans):
        for lo, hi in spans:
            count = (hi - lo) * cap
            lanes = lax.broadcasted_iota(jnp.int32, (mt, count), 1)
            for start in (lo, col + lo):
                choose = jnp.where(lanes + start * cap == tcol[at, 0:1], 1.0, 0.0)
                total = total + jnp.dot(
                    choose.astype(jnp.bfloat16),
                    ret[start : start + hi - lo].reshape(count, 2 * kv_local),
                    preferred_element_type=jnp.float32,
                )
        return total

    def give(*spans):
        def part(i, _):
            at = pl.ds(pl.multiple_of(i * mt, mt), mt)
            acc[at, :] = given(at, acc[at, :], spans)
            return 0

        lax.fori_loop(0, rows // mt, part, 0)

    def join(i, _):
        at = pl.ds(pl.multiple_of(i * tile, tile), tile)
        square = sq_out[0:1, at]
        for m in range(tensors - 1):
            square = square + sq_in[m, 0:1, at]
        scale_row = lax.rsqrt(square / (width * tensors) + epsilon)
        scale_t[at, :] = jnp.broadcast_to(scale_row, (tile, tile)).T
        acc[at, :] = acc[at, :] + base_in[2, at, :].astype(jnp.float32)
        return 0

    def relay(l):
        @pl.when(is_mid)
        def _():
            for h in range(HALVES):
                own_send(l, h).start()

    pump(10)
    pump(0)
    base(far_mate, base_to(0))
    base_copies[0].start()
    base(mate, base_to(1))
    base_copies[1].start()
    for load in own_loads:
        load.wait()
    for l in range(per):
        lower(first + l)
    pump(11)
    base_copies[0].wait_recv()
    base(far, base_sum)
    base_copies[2].start()
    base_copies[1].wait_recv()
    base(me_t, base_own)
    send_on(("moved", 1), ("own", 2))
    pump(1)

    @pl.when(is_mid)
    def _():
        up_arrived(3).wait_recv()
        up_forward(3).start()

    up_load.wait()
    for l in range(per):
        raise_back(first + l)
    lax.fori_loop(0, rows // tile, tables, 0)
    send_on(("moved", 2), ("own", 3))
    mid(lambda: lower(0))
    lower_far(10)
    send_on(("moved", 3))

    @pl.when(is_mid)
    def _():
        lower(1)
        lower_moved(0)

    pump(12)
    lower_far(11)
    send_on(("moved", 5), ("moved", 4))
    mid(lambda: lower_moved(1))
    lower_far(12)
    pump(13)
    pump(2)
    relay(1)
    lower_far(13)
    mid(lambda: lower(2))

    @pl.when(is_end)
    def _():
        up_arrived(2).wait_recv()

    mid(lambda: raise_back(0))
    raise_back(10)
    for copy in sq_copies:
        copy.wait_recv()
    base_copies[2].wait_recv()
    lax.fori_loop(0, rows // tile, join, 0)
    raise_back(11)

    @pl.when(is_mid)
    def _():
        raise_back(1)
        raise_moved(0)
        raise_moved(1)

    @pl.when(is_end)
    def _():
        up_arrived(3).wait_recv()

    raise_back(12)
    mid(lambda: lower_moved(2))
    pump(14)
    lower_far(14)
    raise_back(13)
    mid(lambda: raise_back(2))
    mid(lambda: raise_moved(2))
    pump(3)
    relay(0)
    mid(lambda: lower(3))
    raise_back(14)
    pump(9)

    @pl.when(is_mid)
    def _():
        lower(9)
        raise_back(3)
        lower_moved(3)
        raise_back(9)

    pump(15)
    lower_far(15)

    @pl.when(is_mid)
    def _():
        raise_moved(3)
        lower_moved(5)

    last = 2 * per
    shared = [k for k in range(col) if k < per or k >= per + moved]
    for k in shared[:-1]:
        ret_copy(k).wait_recv()

    @pl.when(is_mid)
    def _():
        for k in range(per, last):
            ret_copy(k).wait_recv()

    @pl.when(is_end)
    def _():
        for j in range(per):
            for cross in range(2):
                moved_copy(j, cross).wait_recv()

    give((0, last), (last + 2, col - 1))
    raise_back(15)
    mid(lambda: raise_moved(5))
    ret_copy(15).wait_recv()

    @pl.when(is_mid)
    def _():
        ret_copy(last + 1).wait_recv()

    @pl.when(is_end)
    def _():
        for cross in range(2):
            moved_copy(per + 1, cross).wait_recv()

    give((last + 1, last + 2), (col - 1, col))

    @pl.when(is_mid)
    def _():
        for h in range(HALVES):
            arrived(last, h).wait_recv()
        lower(last)
        lower_moved(per)
        raise_moved(per)
        raise_back(last)
        ret_copy(last).wait_recv()

    @pl.when(is_end)
    def _():
        for cross in range(2):
            moved_copy(per, cross).wait_recv()

    def finish(i, _):
        at = pl.ds(pl.multiple_of(i * mt, mt), mt)
        total = given(at, acc[at, :], ((last, last + 1),)) * scale_t[at, 0:1]
        c = cos_t[at, :]
        s = sin_t[at, :]
        for head in range(kv_local // HEAD):
            x = total[:, head * HEAD : (head + 1) * HEAD]
            r = x * c + pltpu.roll(x, HEAD // 2, 1) * s
            out[at, head * HEAD : (head + 1) * HEAD] = r.astype(jnp.bfloat16)
        out[at, kv_local:] = total[:, kv_local:].astype(jnp.bfloat16)
        return 0

    lax.fori_loop(0, rows // mt, finish, 0)

    for copy in sq_copies + base_copies:
        copy.wait_send()
    up_send().wait_send()
    for l in range(per):
        for h in range(HALVES):
            own_send(l, h).wait_send()
    for k in range(col):
        y_copy(k).wait_send()

    def sent(k):
        ret_copy(k).wait_send()
        for m in range(1, tensors):
            low_copy(k, m).wait_send()

    for k in shared:
        sent(k)

    @pl.when(is_mid)
    def _():
        for k in forwarded:
            for h in range(HALVES):
                forward(k, h).wait_send()
        for q in (0, 2, 3):
            up_forward(q).wait_send()
        for k in range(per, per + moved):
            sent(k)
        for j in range(moved):
            for m in range(1, tensors):
                low_copy(col + j, m).wait_send()
            for cross in range(2):
                moved_copy(j, cross).wait_send()

    @pl.when(is_end)
    def _():
        for j in range(moved):
            t_copy(j).wait_send()


def fused(
    tokens,
    norm_gain,
    kv_weight,
    adapter_down,
    adapter_up,
    token_adapters,
    adapter_slot,
    request_lengths,
):
    rows, width = tokens.shape
    capacity = max(2, 5 * rows // (4 * adapter_slot.shape[0]))
    cap = -(-capacity // 16) * 16
    stores = lax.axis_size("store")
    tensors = lax.axis_size("tensor")
    per, _, _, kv_local = adapter_up.shape
    depth = stores // 2
    col = depth * per
    moved = per + 2
    ranks = adapter_down.shape[2]
    vmem = pl.BlockSpec(memory_space=pltpu.VMEM)
    smem = pl.BlockSpec(memory_space=pltpu.SMEM)
    hbm = pl.BlockSpec(memory_space=pl.ANY)
    f32, bf16 = jnp.float32, jnp.bfloat16
    dma = pltpu.SemaphoreType.DMA
    both = pl.pallas_call(
        functools.partial(fused_kernel, stores, tensors, cap),
        out_shape=jax.ShapeDtypeStruct((rows, 2 * kv_local), bf16),
        in_specs=[vmem] * 2 + [smem] * 2 + [hbm] * 4,
        out_specs=vmem,
        scratch_shapes=[
            pltpu.VMEM((1, rows), jnp.int32),
            pltpu.VMEM((rows, 128), jnp.int32),
            pltpu.VMEM((rows, HEAD), f32),
            pltpu.VMEM((rows, HEAD), f32),
            pltpu.VMEM((rows, 128), f32),
            pltpu.VMEM((rows, width), bf16),
            pltpu.VMEM((2, 256, 2, kv_local * tensors), bf16),
            pltpu.VMEM((width, 2 * kv_local * tensors), bf16),
            pltpu.VMEM((col, width, ranks), bf16),
            pltpu.VMEM((depth, per, 2, ADAPTER_RANK, kv_local), bf16),
            pltpu.VMEM((col, 2, cap, width), bf16),
            pltpu.VMEM((col, cap, width), bf16),
            pltpu.VMEM((moved, 2, cap, width), bf16),
            pltpu.VMEM((8, rows), f32),
            pltpu.VMEM((tensors - 1, 8, rows), f32),
            pltpu.VMEM((rows, 2 * kv_local), f32),
            pltpu.VMEM((3, rows, 2 * kv_local), bf16),
            pltpu.VMEM((3, rows, 2 * kv_local), bf16),
            pltpu.VMEM((col + moved, 2 * cap, ranks), f32),
            pltpu.VMEM((col + moved, 2 * cap, ranks), bf16),
            pltpu.VMEM((tensors - 1, col + moved, 2 * cap, ranks), bf16),
            pltpu.VMEM((2 * col, cap, 2 * kv_local), bf16),
            pltpu.VMEM((col, cap, 2 * kv_local), bf16),
            pltpu.VMEM((moved, 2, cap, 2 * kv_local), bf16),
            dma((rows // 128,)),
            dma((2,)),
            dma((per,)),
            dma((1,)),
            dma((tensors - 1,)),
            dma((tensors - 1,)),
            dma((col,)),
            dma((col,)),
            dma((moved,)),
            dma((moved,)),
            dma((per, HALVES)),
            dma((col, HALVES)),
            dma((col, HALVES)),
            dma((1 + depth,)),
            dma((depth,)),
            dma((3,)),
            dma((3,)),
            dma((col + moved, tensors - 1)),
            dma((col + moved, tensors - 1)),
            dma((col,)),
            dma((moved, 2)),
            dma((2 * col,)),
        ],
        compiler_params=pltpu.CompilerParams(
            collective_id=0, has_side_effects=True, vmem_limit_bytes=63 * 1024 * 1024
        ),
    )(
        norm_gain[None, :],
        token_adapters.reshape(1, rows),
        adapter_slot,
        request_lengths,
        tokens,
        adapter_up,
        kv_weight,
        adapter_down,
    )
    return both[:, :kv_local], both[:, kv_local:]


def local(
    tokens,
    norm_gain,
    kv_weight,
    adapter_down,
    adapter_up,
    token_adapters,
    adapter_slot,
    request_lengths,
):
    row_count = tokens.shape[0]
    local_width = tokens.shape[1]
    adapter_total = adapter_slot.shape[0]
    capacity = max(2, 5 * row_count // (4 * adapter_total))
    store_size = lax.axis_size("store")
    per_owner = adapter_down.shape[0]
    kv_local = adapter_up.shape[3]
    widened = tokens.astype(jnp.float32)
    squares = lax.psum(jnp.sum(widened * widened, axis=1), "tensor")
    normed = (widened * lax.rsqrt(squares / D + epsilon)[:, None] * norm_gain[None, :]).astype(
        jnp.bfloat16
    )
    targets = place_rows(token_adapters[:, 0], adapter_slot, capacity)
    send_rows = (
        jnp.zeros((adapter_total * capacity, local_width), jnp.bfloat16).at[targets].set(normed)
    )
    send_rows = send_rows.reshape(store_size, per_owner, capacity, local_width)
    down_projected = jnp.einsum(
        "slcd,ldr->slcr",
        lax.all_to_all(send_rows, "store", split_axis=0, concat_axis=0, tiled=True),
        adapter_down,
        preferred_element_type=jnp.float32,
    )
    rank_total_sum = lax.psum(down_projected, "tensor")
    rank_activation = (rank_total_sum * adapter_scale).astype(jnp.bfloat16)
    split_rank = rank_activation.reshape(rank_activation.shape[:3] + (2, ADAPTER_RANK))
    update_rows = jnp.einsum(
        "slcjr,ljrk->slcjk", split_rank, adapter_up, preferred_element_type=jnp.float32
    )
    back_rows = update_rows.astype(jnp.bfloat16).reshape(
        rank_activation.shape[:3] + (2 * kv_local,)
    )
    returned = lax.all_to_all(back_rows, "store", split_axis=0, concat_axis=0, tiled=True)
    delta_rows = returned.reshape(adapter_total * capacity, 2, kv_local)[targets]
    partial_value = jnp.einsum("td,djk->tjk", normed, kv_weight, preferred_element_type=jnp.float32)
    base_part = lax.psum_scatter(partial_value, "tensor", scatter_dimension=2, tiled=True)
    combined = base_part + delta_rows.astype(jnp.float32)
    positions = positions_of(lax.axis_index("store") * row_count, row_count, request_lengths)
    new_keys = rotate(combined[:, 0, :], positions).astype(jnp.bfloat16)
    new_values = combined[:, 1, :].astype(jnp.bfloat16)
    return (new_keys, new_values)


def solution(mesh):
    small = mesh.shape["store"] == 8 and mesh.shape["tensor"] == 4
    return jax.shard_map(
        fused if small else local,
        mesh=mesh,
        in_specs=(
            P("store", "tensor"),
            P("tensor"),
            P("tensor", None, None),
            P("store", "tensor", None),
            P("store", None, None, "tensor"),
            P("store", None),
            P(),
            P(),
        ),
        out_specs=(P("store", "tensor"), P("store", "tensor")),
        check_vma=False,
    )
```

```python
import functools
import math

import jax
import jax.numpy as jnp
from jax import lax
from jax.experimental import pallas as pl
from jax.experimental.pallas import tpu as pltpu
from jax.sharding import PartitionSpec as P

D = 8192
HEAD = 128
ADAPTER_RANK = 64


epsilon = 1e-05
adapter_scale = 2.0
rope_theta = 500000.0


def place_rows(adapter_ids, adapter_slot, capacity):
    catalog = jnp.arange(adapter_slot.shape[0], dtype=jnp.int32)
    slot_rows = jnp.sum(
        jnp.where(adapter_ids[:, None] == catalog[None, :], adapter_slot[None, :], 0), axis=1
    )
    row_order = jnp.arange(adapter_ids.shape[0], dtype=jnp.int32)
    same_earlier = (adapter_ids[:, None] == adapter_ids[None, :]) & (
        row_order[None, :] < row_order[:, None]
    )
    rank_rows = jnp.sum(same_earlier.astype(jnp.int32), axis=1)
    return slot_rows * capacity + rank_rows


def positions_of(first_row, row_count, lengths):
    global_rows = first_row + jnp.arange(row_count, dtype=jnp.int32)
    request_ends = jnp.cumsum(lengths)
    preceding = jnp.sum(
        jnp.where(request_ends[None, :] <= global_rows[:, None], lengths[None, :], 0), axis=1
    )
    return global_rows - preceding


def rotate(states, positions):
    per_head = states.reshape(states.shape[0], -1, HEAD)
    half_size = HEAD // 2
    frequency = jnp.exp(
        jnp.arange(half_size, dtype=jnp.float32) * (-2.0 * math.log(rope_theta) / HEAD)
    )
    angles = positions.astype(jnp.float32)[:, None] * frequency[None, :]
    cos_part = jnp.concatenate([jnp.cos(angles), jnp.cos(angles)], axis=1)[:, None, :]
    sin_part = jnp.concatenate([jnp.sin(angles), jnp.sin(angles)], axis=1)[:, None, :]
    low_half = per_head[..., :half_size]
    high_half = per_head[..., half_size:]
    turned = jnp.concatenate([-high_half, low_half], axis=-1)
    return (per_head * cos_part + turned * sin_part).reshape(states.shape)


MESH = pl.DeviceIdType.MESH


HALVES = 2


def fused_kernel(
    stores,
    tensors,
    cap,
    gain,
    ids,
    slots,
    lengths,
    tok_hbm,
    up_hbm,
    w_hbm,
    down_hbm,
    out_hbm,
    out,
    trow,
    tcol,
    cos_t,
    sin_t,
    scale_t,
    g,
    w3,
    w,
    down,
    up,
    own,
    snd,
    tin,
    sq_out,
    sq_in,
    acc,
    base_out,
    base_in,
    low_own,
    low_out,
    low_in,
    ret,
    ret_y,
    ret_t,
    tl_sem,
    w_sem,
    ld_sem,
    lu_sem,
    sq_ss,
    sq_rs,
    y_ss,
    y_rs,
    t_ss,
    t_rs,
    dn_ss,
    dn_fs,
    dn_rs,
    up_ss,
    up_fs,
    up_rs,
    base_ss,
    base_rs,
    low_ss,
    low_rs,
    ret_ss,
    rt_ss,
    ret_rs,
    out_sem,
):
    rows, width = tok_hbm.shape
    per = down_hbm.shape[0]
    depth = stores // 2
    col = depth * per
    moved = per + 2
    kv_local = up.shape[4]
    kv_whole = kv_local * tensors
    half_rows = width // HALVES
    me_s = lax.axis_index("store")
    me_t = lax.axis_index("tensor")
    z = me_s // 2
    y = me_s % 2
    low_side = z < 2
    is_mid = (z == 1) | (z == 2)
    is_end = (z == 0) | (z == 3)
    across = 3 - z
    inner = jnp.where(low_side, 1, 2)
    outer = jnp.where(low_side, 0, 3)
    z_next = jnp.where(is_mid, across, inner)
    first = jnp.where(is_mid, per, 0)

    def remote(src, dst, ss, rs, store, tensor):
        return pltpu.make_async_remote_copy(
            src_ref=src, dst_ref=dst, send_sem=ss, recv_sem=rs,
            device_id={"store": store, "tensor": tensor}, device_id_type=MESH,
        )

    def to_tensor(step):
        return (me_t + step) % tensors

    mate = me_t // 2 * 2 + 1 - me_t % 2
    far = (me_t + 2) % tensors
    far_mate = (mate + 2) % tensors
    beside = z * 2 + 1 - y

    def part_of(h):
        return pl.ds(h * half_rows, half_rows)

    tile = 128
    tok_loads = [
        pltpu.make_async_copy(
            tok_hbm.at[pl.ds(i * tile, tile)], g.at[pl.ds(i * tile, tile)], tl_sem.at[i]
        )
        for i in range(rows // tile)
    ]
    for load in tok_loads:
        load.start()
    wt = w3.shape[1]
    w_loads = [
        pltpu.make_async_copy(w_hbm.at[pl.ds(i * wt, wt)], w3.at[i % 2], w_sem.at[i % 2])
        for i in range(width // wt)
    ]
    own_loads = [
        pltpu.make_async_copy(down_hbm.at[l], down.at[first + l], ld_sem.at[l]) for l in range(per)
    ]
    up_load = pltpu.make_async_copy(up_hbm, up.at[first // per], lu_sem.at[0])

    barrier = pltpu.get_barrier_semaphore()

    def greet(store, tensor):
        pl.semaphore_signal(
            barrier, inc=1, device_id={"store": store, "tensor": tensor}, device_id_type=MESH
        )

    for step in range(1, tensors):
        greet(me_s, to_tensor(step))
    greet(beside, me_t)

    @pl.when(is_mid)
    def _():
        greet(across * 2 + y, me_t)
        for side in range(2):
            greet(outer * 2 + side, me_t)

    @pl.when(is_end)
    def _():
        for side in range(2):
            greet(inner * 2 + side, me_t)

    w_loads[0].start()
    w_loads[1].start()
    for load in own_loads:
        load.start()
    up_load.start()

    @pl.when(is_mid)
    def _():
        pl.semaphore_wait(barrier, tensors + 3)

    @pl.when(is_end)
    def _():
        pl.semaphore_wait(barrier, tensors + 2)


    def own_send(l, h):
        k = jnp.where(is_mid, 2 * per + l, l)
        return remote(
            down_hbm.at[l, part_of(h)], down.at[k, part_of(h)], dn_ss.at[l, h], dn_rs.at[k, h],
            z_next * 2 + y, me_t,
        )

    def up_send():
        return remote(up_hbm, up.at[0], up_ss.at[0], up_rs.at[0], z_next * 2 + y, me_t)

    def up_part(late):
        part = pl.ds(0, 1) if late else pl.ds(1, per - 1)
        n = depth if late else 2
        return remote(
            up_hbm.at[part], up.at[2, part], up_ss.at[1 + n], up_rs.at[n], across * 2 + y, me_t
        )

    def forward(k, h):
        if k < per:
            to, at = across, k + 3 * per
        else:
            to, at = outer, k
        return remote(
            down.at[k, part_of(h)], down.at[at, part_of(h)], dn_fs.at[k, h], dn_rs.at[at, h],
            to * 2 + y, me_t,
        )

    def up_forward(q):
        to, at = (across, 3) if q == 0 else (outer, q)
        src, dst = up.at[q], up.at[at]
        if q == 2:
            part = pl.ds(moved - per, 2 * per - moved)
            src, dst = up.at[q, part], up.at[at, part]
        return remote(src, dst, up_fs.at[q], up_rs.at[at], to * 2 + y, me_t)

    def arrived(k, h):
        return remote(
            down.at[k, part_of(h)], down.at[k, part_of(h)], dn_fs.at[k, h], dn_rs.at[k, h],
            z_next * 2 + y, me_t,
        )

    def up_arrived(q):
        return remote(up.at[q], up.at[q], up_fs.at[q], up_rs.at[q], z_next * 2 + y, me_t)

    forwarded = [k for k in range(col) if not per <= k < per + moved]

    @pl.when(is_mid)
    def _():
        up_part(0).start()
        for l in (2, 3):
            for h in range(HALVES):
                own_send(l, h).start()

    @pl.when(is_end)
    def _():
        up_send().start()
        for h in range(HALVES):
            own_send(0, h).start()

    adapters = slots.shape[0]
    named = jnp.where(
        lax.broadcasted_iota(jnp.int32, (adapters, rows), 0) == ids[...], 1.0, 0.0
    )
    earlier = jnp.where(
        lax.broadcasted_iota(jnp.int32, (rows, rows), 0)
        < lax.broadcasted_iota(jnp.int32, (rows, rows), 1),
        1.0,
        0.0,
    ).astype(jnp.bfloat16)
    counts = jnp.dot(named.astype(jnp.bfloat16), earlier, preferred_element_type=jnp.float32)
    rank = jnp.sum(named * counts, axis=0, keepdims=True).astype(jnp.int32)
    slot = jnp.zeros((1, rows), jnp.int32)
    for a in range(adapters):
        slot = jnp.where(ids[...] == a, slots[a], slot)
    owner = slot // per
    plane = owner // 2
    place = jnp.where(low_side, plane, depth - 1 - plane) * per + slot % per
    other = jnp.where(owner % 2 == y, 0, col)
    trow[...] = (other + place) * cap + rank

    def scale(i, _):
        at = pl.ds(pl.multiple_of(i * tile, tile), tile)
        pltpu.make_async_copy(tok_hbm.at[at], g.at[at], tl_sem.at[i]).wait()
        x = g[at, :].astype(jnp.float32)
        g[at, :] = (x * gain[...]).astype(jnp.bfloat16)
        total = x[:, 0:128] * x[:, 0:128]
        for lane in range(1, width // 128):
            part = x[:, lane * 128 : (lane + 1) * 128]
            total = total + part * part
        sq_out[:, at] = jnp.broadcast_to(jnp.sum(total.T, axis=0, keepdims=True), (8, tile))
        return 0

    lax.fori_loop(0, rows // tile, scale, 0)

    sq_copies = [
        remote(sq_out, sq_in.at[m - 1], sq_ss.at[m - 1], sq_rs.at[m - 1], me_s, to_tensor(m))
        for m in range(1, tensors)
    ]
    for copy in sq_copies:
        copy.start()

    chunk = 512
    batch = col // 2

    def pick(group, store):
        places = lax.broadcasted_iota(jnp.int32, (batch * cap, rows), 0) + group * cap
        choose = jnp.where(places == trow[...], 1.0, 0.0).astype(jnp.bfloat16)

        def part(i, _):
            at = pl.ds(pl.multiple_of(i * chunk, chunk), chunk)
            r = jnp.dot(choose, g[:, at], preferred_element_type=jnp.float32)
            store(at, r.astype(jnp.bfloat16).reshape(batch, cap, chunk))
            return 0

        lax.fori_loop(0, width // chunk, part, 0)

    def y_copy(k):
        return remote(snd.at[k], own.at[k, 1], y_ss.at[k], y_rs.at[k], beside, me_t)

    def t_copy(j):
        return remote(
            own.at[per + j], tin.at[j], t_ss.at[j], t_rs.at[j], inner * 2 + y, me_t
        )

    for b in range(2):
        def to_snd(at, r, b=b):
            snd[b * batch : (b + 1) * batch, :, at] = r

        pick(col + b * batch, to_snd)

    mid_order = [4, 5, 6, 7, 10, 0, 11, 1, 12, 13, 2, 14, 3, 9, 15, 8]
    end_order = [4, 5, 0, 1, 2, 3, 6, 10, 7, 11, 8, 9, 12, 13, 14, 15]

    @pl.when(is_mid)
    def _():
        for k in mid_order:
            y_copy(k).start()

    @pl.when(is_end)
    def _():
        for k in end_order:
            y_copy(k).start()

    for b in range(2):
        def to_own(at, r, b=b):
            own[b * batch : (b + 1) * batch, 0, :, at] = r

        pick(b * batch, to_own)

    def mid(body):
        pl.when(is_mid)(body)

    def pump(k, halves=range(HALVES)):
        def body():
            for h in halves:
                arrived(k, h).wait_recv()
                if k in forwarded:
                    forward(k, h).start()

        mid(body)

    def pump_up(q):
        def body():
            if q == 2:
                up_part(0).wait_recv()
            else:
                up_arrived(q).wait_recv()
            up_forward(q).start()

        mid(body)

    def send_on(*moves):
        def body():
            for kind, n in moves:
                if kind == "own":
                    for h in range(HALVES):
                        own_send(n, h).start()
                else:
                    y_copy(per + n).wait_recv()
                    t_copy(n).start()

        pl.when(is_end)(body)

    send_on(("moved", 0), ("own", 1))
    pump_up(2)
    pump_up(0)

    dt = 128
    two = lax.broadcasted_iota(jnp.int32, (dt, 2 * dt), 1) - 2 * lax.broadcasted_iota(
        jnp.int32, (dt, 2 * dt), 0
    )
    every = [jnp.where(two == j, 1.0, 0.0).astype(jnp.bfloat16) for j in range(2)]
    for i in range(width // wt):
        w_loads[i].wait()

        def part_kinds(n, _, i=i):
            x = w3[i % 2, pl.ds(pl.multiple_of(n * dt, dt), dt)].reshape(2 * dt, kv_whole)
            at = pl.ds(pl.multiple_of(i * wt + n * dt, dt), dt)
            for j in range(2):
                w[at, j * kv_whole : (j + 1) * kv_whole] = jnp.dot(
                    every[j], x, preferred_element_type=jnp.float32
                ).astype(jnp.bfloat16)
            return 0

        lax.fori_loop(0, wt // dt, part_kinds, 0)
        if i + 2 < width // wt:
            w_loads[i + 2].start()

    mt = 256
    base_copies = [
        remote(base_out.at[n], base_in.at[n], base_ss.at[n], base_rs.at[n], me_s, to)
        for n, to in enumerate((mate, mate, far))
    ]

    def base(target, store):
        for j in range(2):
            cols = pl.ds(pl.multiple_of(j * kv_whole + target * kv_local, kv_local), kv_local)

            def part(i, _, j=j, cols=cols):
                at = pl.ds(pl.multiple_of(i * mt, mt), mt)
                r = jnp.dot(g[at, :], w[:, cols], preferred_element_type=jnp.float32)
                store(at, slice(j * kv_local, (j + 1) * kv_local), r)
                return 0

            lax.fori_loop(0, rows // mt, part, 0)

    def base_to(n):
        def store(at, cols, r):
            base_out[n, at, cols] = r.astype(jnp.bfloat16)

        return store

    def base_sum(at, cols, r):
        base_out[2, at, cols] = (r + base_in[0, at, cols].astype(jnp.float32)).astype(jnp.bfloat16)

    def base_own(at, cols, r):
        acc[at, cols] = r + base_in[1, at, cols].astype(jnp.float32)

    half = HEAD // 2
    lane = lax.broadcasted_iota(jnp.int32, (1, HEAD), 1)
    frequency = jnp.exp(
        (lane % half).astype(jnp.float32) * (-2.0 * math.log(rope_theta) / HEAD)
    )
    sign = jnp.where(lane < half, -1.0, 1.0)

    def tables(i, _):
        at = pl.ds(pl.multiple_of(i * tile, tile), tile)
        row = lax.broadcasted_iota(jnp.int32, (tile, HEAD), 0) + (me_s * rows + i * tile)
        position = row
        end = 0
        for r in range(lengths.shape[0]):
            end = end + lengths[r]
            position = jnp.where(row >= end, row - end, position)
        angles = position.astype(jnp.float32) * frequency
        cos_t[at, :] = jnp.cos(angles)
        sin_t[at, :] = jnp.sin(angles) * sign
        tcol[at, :] = jnp.broadcast_to(trow[:, at], (tile, tile)).T
        return 0

    def low_copy(n, m):
        return remote(
            low_out.at[n], low_in.at[m - 1, n], low_ss.at[n, m - 1], low_rs.at[n, m - 1],
            me_s, to_tensor(m),
        )

    def lower_rows(n, k, x):
        r = jnp.dot(x, down[k], preferred_element_type=jnp.float32)
        low_own[n] = r
        low_out[n] = r.astype(jnp.bfloat16)
        for m in range(1, tensors):
            low_copy(n, m).start()

    def lower(k):
        y_copy(k).wait_recv()
        lower_rows(k, k, own[k].reshape(2 * cap, width))

    def lower_moved(j):
        t_copy(j).wait_recv()
        lower_rows(col + j, per + j, tin[j].reshape(2 * cap, width))

    def raised(n, k):
        total = low_own[n]
        for m in range(1, tensors):
            low_copy(n, m).wait_recv()
            total = total + low_in[m - 1, n].astype(jnp.float32)
        middle = (total * adapter_scale).astype(jnp.bfloat16)
        return [
            jnp.dot(
                middle[:, j * ADAPTER_RANK : (j + 1) * ADAPTER_RANK],
                up[k // per, k % per, j],
                preferred_element_type=jnp.float32,
            ).astype(jnp.bfloat16)
            for j in range(2)
        ]

    def ret_copy(k):
        return remote(
            ret_y.at[k], ret.at[col + k], ret_ss.at[k], ret_rs.at[col + k], beside, me_t
        )

    def moved_copy(j, cross):
        at = per + j + (col if cross else 0)
        to = outer * 2 + (1 - y if cross else y)
        return remote(ret_t.at[j, cross], ret.at[at], rt_ss.at[j, cross], ret_rs.at[at], to, me_t)

    def raise_back(k):
        for j, d in enumerate(raised(k, k)):
            cols = slice(j * kv_local, (j + 1) * kv_local)
            ret[k, :, cols] = d[:cap]
            ret_y[k, :, cols] = d[cap:]
        ret_copy(k).start()

    def raise_moved(n):
        for j, d in enumerate(raised(col + n, per + n)):
            cols = slice(j * kv_local, (j + 1) * kv_local)
            ret_t[n, 0, :, cols] = d[:cap]
            ret_t[n, 1, :, cols] = d[cap:]
        moved_copy(n, 0).start()
        moved_copy(n, 1).start()

    def lower_far(k):
        @pl.when(is_end)
        def _():
            for h in range(HALVES):
                arrived(k, h).wait_recv()

        lower(k)

    def given(at, total, spans):
        for lo, hi in spans:
            count = (hi - lo) * cap
            lanes = lax.broadcasted_iota(jnp.int32, (mt, count), 1)
            for start in (lo, col + lo):
                choose = jnp.where(lanes + start * cap == tcol[at, 0:1], 1.0, 0.0)
                total = total + jnp.dot(
                    choose.astype(jnp.bfloat16),
                    ret[start : start + hi - lo].reshape(count, 2 * kv_local),
                    preferred_element_type=jnp.float32,
                )
        return total

    def give(*spans):
        def part(i, _):
            at = pl.ds(pl.multiple_of(i * mt, mt), mt)
            acc[at, :] = given(at, acc[at, :], spans)
            return 0

        lax.fori_loop(0, rows // mt, part, 0)

    def join(i, _):
        at = pl.ds(pl.multiple_of(i * tile, tile), tile)
        square = sq_out[0:1, at]
        for m in range(tensors - 1):
            square = square + sq_in[m, 0:1, at]
        scale_row = lax.rsqrt(square / (width * tensors) + epsilon)
        scale_t[at, :] = jnp.broadcast_to(scale_row, (tile, tile)).T
        acc[at, :] = acc[at, :] + base_in[2, at, :].astype(jnp.float32)
        return 0

    def relay(l):
        @pl.when(is_mid)
        def _():
            for h in range(HALVES):
                own_send(l, h).start()

    pump(10)
    pump(0)
    base(far_mate, base_to(0))
    base_copies[0].start()
    base(mate, base_to(1))
    base_copies[1].start()
    send_on(("moved", 1), ("own", 2), ("own", 3))
    for load in own_loads:
        load.wait()
    for l in range(per):
        lower(first + l)
    pump(11)
    base_copies[0].wait_recv()
    base(far, base_sum)
    base_copies[2].start()
    base_copies[1].wait_recv()
    base(me_t, base_own)
    pump(1)

    @pl.when(is_mid)
    def _():
        up_arrived(3).wait_recv()
        up_forward(3).start()

    up_load.wait()
    for l in range(per):
        raise_back(first + l)
    lax.fori_loop(0, rows // tile, tables, 0)
    send_on(("moved", 2))
    mid(lambda: lower(0))
    lower_far(10)
    send_on(("moved", 3))

    @pl.when(is_mid)
    def _():
        lower(1)
        lower_moved(0)

    pump(12)
    lower_far(11)
    send_on(("moved", 4), ("moved", 5))
    mid(lambda: lower_moved(1))
    lower_far(12)
    pump(13, [0])
    pump(2)
    relay(1)
    pump(13, range(1, HALVES))
    lower_far(13)
    mid(lambda: lower(2))

    @pl.when(is_end)
    def _():
        up_forward(2).wait_recv()

    mid(lambda: raise_back(0))
    raise_back(10)
    for copy in sq_copies:
        copy.wait_recv()
    base_copies[2].wait_recv()
    lax.fori_loop(0, rows // tile, join, 0)
    raise_back(11)

    @pl.when(is_mid)
    def _():
        raise_back(1)
        raise_moved(0)
        raise_moved(1)

    @pl.when(is_end)
    def _():
        up_arrived(3).wait_recv()

    raise_back(12)
    pump(14)
    pump(3)
    relay(0)
    mid(lambda: up_part(1).start())
    lower_far(14)
    mid(lambda: lower(3))
    raise_back(13)
    mid(lambda: raise_back(2))
    mid(lambda: lower_moved(2))
    raise_back(14)
    pump(9)

    @pl.when(is_mid)
    def _():
        lower(9)
        raise_back(3)
        raise_moved(2)
        lower_moved(3)
        raise_back(9)

    pump(15)
    lower_far(15)

    @pl.when(is_mid)
    def _():
        raise_moved(3)
        lower_moved(5)

    last = 2 * per
    shared = [k for k in range(col) if k < per or k >= per + moved]
    for k in shared[:-1]:
        ret_copy(k).wait_recv()

    @pl.when(is_mid)
    def _():
        for k in range(per, last):
            ret_copy(k).wait_recv()

    @pl.when(is_end)
    def _():
        for j in range(per):
            for cross in range(2):
                moved_copy(j, cross).wait_recv()

    give((0, last), (last + 2, col - 1))
    raise_back(15)
    mid(lambda: raise_moved(5))
    ret_copy(15).wait_recv()

    @pl.when(is_mid)
    def _():
        ret_copy(last + 1).wait_recv()

    @pl.when(is_end)
    def _():
        for cross in range(2):
            moved_copy(per + 1, cross).wait_recv()

    give((last + 1, last + 2), (col - 1, col))

    @pl.when(is_mid)
    def _():
        for h in range(HALVES):
            arrived(last, h).wait_recv()
        lower(last)
        lower_moved(per)
        up_part(1).wait_recv()
        raise_moved(per)
        raise_back(last)
        ret_copy(last).wait_recv()

    @pl.when(is_end)
    def _():
        for cross in range(2):
            moved_copy(per, cross).wait_recv()

    def finish(i, _):
        at = pl.ds(pl.multiple_of(i * mt, mt), mt)
        total = given(at, acc[at, :], ((last, last + 1),)) * scale_t[at, 0:1]
        c = cos_t[at, :]
        s = sin_t[at, :]
        for head in range(kv_local // HEAD):
            x = total[:, head * HEAD : (head + 1) * HEAD]
            r = x * c + pltpu.roll(x, HEAD // 2, 1) * s
            out[at, head * HEAD : (head + 1) * HEAD] = r.astype(jnp.bfloat16)
        out[at, kv_local:] = total[:, kv_local:].astype(jnp.bfloat16)
        pltpu.make_async_copy(out.at[at], out_hbm.at[at], out_sem.at[i]).start()
        return 0

    lax.fori_loop(0, rows // mt, finish, 0)

    for copy in sq_copies + base_copies:
        copy.wait_send()
    for l in range(per):
        for h in range(HALVES):
            own_send(l, h).wait_send()
    for k in range(col):
        y_copy(k).wait_send()

    def sent(k):
        ret_copy(k).wait_send()
        for m in range(1, tensors):
            low_copy(k, m).wait_send()

    for k in shared:
        sent(k)

    @pl.when(is_mid)
    def _():
        for k in forwarded:
            for h in range(HALVES):
                forward(k, h).wait_send()
        for q in (0, 2, 3):
            up_forward(q).wait_send()
        up_part(0).wait_send()
        up_part(1).wait_send()
        for k in range(per, per + moved):
            sent(k)
        for j in range(moved):
            for m in range(1, tensors):
                low_copy(col + j, m).wait_send()
            for cross in range(2):
                moved_copy(j, cross).wait_send()

    for i in range(rows // mt):
        at = pl.ds(i * mt, mt)
        pltpu.make_async_copy(out.at[at], out_hbm.at[at], out_sem.at[i]).wait()

    @pl.when(is_end)
    def _():
        up_send().wait_send()
        for j in range(moved):
            t_copy(j).wait_send()


def fused(
    tokens,
    norm_gain,
    kv_weight,
    adapter_down,
    adapter_up,
    token_adapters,
    adapter_slot,
    request_lengths,
):
    rows, width = tokens.shape
    capacity = max(2, 5 * rows // (4 * adapter_slot.shape[0]))
    cap = -(-capacity // 8) * 8
    stores = lax.axis_size("store")
    tensors = lax.axis_size("tensor")
    per, _, _, kv_local = adapter_up.shape
    depth = stores // 2
    col = depth * per
    moved = per + 2
    ranks = adapter_down.shape[2]
    vmem = pl.BlockSpec(memory_space=pltpu.VMEM)
    smem = pl.BlockSpec(memory_space=pltpu.SMEM)
    hbm = pl.BlockSpec(memory_space=pl.ANY)
    f32, bf16 = jnp.float32, jnp.bfloat16
    dma = pltpu.SemaphoreType.DMA
    both = pl.pallas_call(
        functools.partial(fused_kernel, stores, tensors, cap),
        out_shape=jax.ShapeDtypeStruct((rows, 2 * kv_local), bf16),
        in_specs=[vmem] * 2 + [smem] * 2 + [hbm] * 4,
        out_specs=hbm,
        scratch_shapes=[
            pltpu.VMEM((rows, 2 * kv_local), bf16),
            pltpu.VMEM((1, rows), jnp.int32),
            pltpu.VMEM((rows, 128), jnp.int32),
            pltpu.VMEM((rows, HEAD), f32),
            pltpu.VMEM((rows, HEAD), f32),
            pltpu.VMEM((rows, 128), f32),
            pltpu.VMEM((rows, width), bf16),
            pltpu.VMEM((2, 256, 2, kv_local * tensors), bf16),
            pltpu.VMEM((width, 2 * kv_local * tensors), bf16),
            pltpu.VMEM((col, width, ranks), bf16),
            pltpu.VMEM((depth, per, 2, ADAPTER_RANK, kv_local), bf16),
            pltpu.VMEM((col, 2, cap, width), bf16),
            pltpu.VMEM((col, cap, width), bf16),
            pltpu.VMEM((moved, 2, cap, width), bf16),
            pltpu.VMEM((8, rows), f32),
            pltpu.VMEM((tensors - 1, 8, rows), f32),
            pltpu.VMEM((rows, 2 * kv_local), f32),
            pltpu.VMEM((3, rows, 2 * kv_local), bf16),
            pltpu.VMEM((3, rows, 2 * kv_local), bf16),
            pltpu.VMEM((col + moved, 2 * cap, ranks), f32),
            pltpu.VMEM((col + moved, 2 * cap, ranks), bf16),
            pltpu.VMEM((tensors - 1, col + moved, 2 * cap, ranks), bf16),
            pltpu.VMEM((2 * col, cap, 2 * kv_local), bf16),
            pltpu.VMEM((col, cap, 2 * kv_local), bf16),
            pltpu.VMEM((moved, 2, cap, 2 * kv_local), bf16),
            dma((rows // 128,)),
            dma((2,)),
            dma((per,)),
            dma((1,)),
            dma((tensors - 1,)),
            dma((tensors - 1,)),
            dma((col,)),
            dma((col,)),
            dma((moved,)),
            dma((moved,)),
            dma((per, HALVES)),
            dma((col, HALVES)),
            dma((col, HALVES)),
            dma((2 + depth,)),
            dma((depth,)),
            dma((1 + depth,)),
            dma((3,)),
            dma((3,)),
            dma((col + moved, tensors - 1)),
            dma((col + moved, tensors - 1)),
            dma((col,)),
            dma((moved, 2)),
            dma((2 * col,)),
            dma((rows // 256,)),
        ],
        compiler_params=pltpu.CompilerParams(
            collective_id=0, has_side_effects=True, vmem_limit_bytes=63 * 1024 * 1024
        ),
    )(
        norm_gain[None, :],
        token_adapters.reshape(1, rows),
        adapter_slot,
        request_lengths,
        tokens,
        adapter_up,
        kv_weight,
        adapter_down,
    )
    return both[:, :kv_local], both[:, kv_local:]


def local(
    tokens,
    norm_gain,
    kv_weight,
    adapter_down,
    adapter_up,
    token_adapters,
    adapter_slot,
    request_lengths,
):
    row_count = tokens.shape[0]
    local_width = tokens.shape[1]
    adapter_total = adapter_slot.shape[0]
    capacity = max(2, 5 * row_count // (4 * adapter_total))
    store_size = lax.axis_size("store")
    per_owner = adapter_down.shape[0]
    kv_local = adapter_up.shape[3]
    widened = tokens.astype(jnp.float32)
    squares = lax.psum(jnp.sum(widened * widened, axis=1), "tensor")
    normed = (widened * lax.rsqrt(squares / D + epsilon)[:, None] * norm_gain[None, :]).astype(
        jnp.bfloat16
    )
    targets = place_rows(token_adapters[:, 0], adapter_slot, capacity)
    send_rows = (
        jnp.zeros((adapter_total * capacity, local_width), jnp.bfloat16).at[targets].set(normed)
    )
    send_rows = send_rows.reshape(store_size, per_owner, capacity, local_width)
    down_projected = jnp.einsum(
        "slcd,ldr->slcr",
        lax.all_to_all(send_rows, "store", split_axis=0, concat_axis=0, tiled=True),
        adapter_down,
        preferred_element_type=jnp.float32,
    )
    rank_total_sum = lax.psum(down_projected, "tensor")
    rank_activation = (rank_total_sum * adapter_scale).astype(jnp.bfloat16)
    split_rank = rank_activation.reshape(rank_activation.shape[:3] + (2, ADAPTER_RANK))
    update_rows = jnp.einsum(
        "slcjr,ljrk->slcjk", split_rank, adapter_up, preferred_element_type=jnp.float32
    )
    back_rows = update_rows.astype(jnp.bfloat16).reshape(
        rank_activation.shape[:3] + (2 * kv_local,)
    )
    returned = lax.all_to_all(back_rows, "store", split_axis=0, concat_axis=0, tiled=True)
    delta_rows = returned.reshape(adapter_total * capacity, 2, kv_local)[targets]
    partial_value = jnp.einsum("td,djk->tjk", normed, kv_weight, preferred_element_type=jnp.float32)
    base_part = lax.psum_scatter(partial_value, "tensor", scatter_dimension=2, tiled=True)
    combined = base_part + delta_rows.astype(jnp.float32)
    positions = positions_of(lax.axis_index("store") * row_count, row_count, request_lengths)
    new_keys = rotate(combined[:, 0, :], positions).astype(jnp.bfloat16)
    new_values = combined[:, 1, :].astype(jnp.bfloat16)
    return (new_keys, new_values)


def solution(mesh):
    small = mesh.shape["store"] == 8 and mesh.shape["tensor"] == 4
    return jax.shard_map(
        fused if small else local,
        mesh=mesh,
        in_specs=(
            P("store", "tensor"),
            P("tensor"),
            P("tensor", None, None),
            P("store", "tensor", None),
            P("store", None, None, "tensor"),
            P("store", None),
            P(),
            P(),
        ),
        out_specs=(P("store", "tensor"), P("store", "tensor")),
        check_vma=False,
    )
```

```python
import functools
import math

import jax
import jax.numpy as jnp
from jax import lax
from jax.experimental import pallas as pl
from jax.experimental.pallas import tpu as pltpu
from jax.sharding import PartitionSpec as P

D = 8192
HEAD = 128
ADAPTER_RANK = 64


epsilon = 1e-05
adapter_scale = 2.0
rope_theta = 500000.0


def place_rows(adapter_ids, adapter_slot, capacity):
    catalog = jnp.arange(adapter_slot.shape[0], dtype=jnp.int32)
    slot_rows = jnp.sum(
        jnp.where(adapter_ids[:, None] == catalog[None, :], adapter_slot[None, :], 0), axis=1
    )
    row_order = jnp.arange(adapter_ids.shape[0], dtype=jnp.int32)
    same_earlier = (adapter_ids[:, None] == adapter_ids[None, :]) & (
        row_order[None, :] < row_order[:, None]
    )
    rank_rows = jnp.sum(same_earlier.astype(jnp.int32), axis=1)
    return slot_rows * capacity + rank_rows


def positions_of(first_row, row_count, lengths):
    global_rows = first_row + jnp.arange(row_count, dtype=jnp.int32)
    request_ends = jnp.cumsum(lengths)
    preceding = jnp.sum(
        jnp.where(request_ends[None, :] <= global_rows[:, None], lengths[None, :], 0), axis=1
    )
    return global_rows - preceding


def rotate(states, positions):
    per_head = states.reshape(states.shape[0], -1, HEAD)
    half_size = HEAD // 2
    frequency = jnp.exp(
        jnp.arange(half_size, dtype=jnp.float32) * (-2.0 * math.log(rope_theta) / HEAD)
    )
    angles = positions.astype(jnp.float32)[:, None] * frequency[None, :]
    cos_part = jnp.concatenate([jnp.cos(angles), jnp.cos(angles)], axis=1)[:, None, :]
    sin_part = jnp.concatenate([jnp.sin(angles), jnp.sin(angles)], axis=1)[:, None, :]
    low_half = per_head[..., :half_size]
    high_half = per_head[..., half_size:]
    turned = jnp.concatenate([-high_half, low_half], axis=-1)
    return (per_head * cos_part + turned * sin_part).reshape(states.shape)


MESH = pl.DeviceIdType.MESH


HALVES = 2


def fused_kernel(
    stores,
    tensors,
    cap,
    gain,
    ids,
    slots,
    lengths,
    tok_hbm,
    up_hbm,
    w_hbm,
    down_hbm,
    out_hbm,
    out,
    trow,
    tcol,
    cos_t,
    sin_t,
    scale_t,
    g,
    w3,
    w,
    down,
    up,
    own,
    snd,
    tin,
    sq_out,
    sq_in,
    acc,
    base_out,
    base_in,
    low_own,
    low_out,
    low_in,
    ret,
    ret_y,
    ret_t,
    tl_sem,
    w_sem,
    ld_sem,
    lu_sem,
    sq_ss,
    sq_rs,
    y_ss,
    y_rs,
    t_ss,
    t_rs,
    dn_ss,
    dn_fs,
    dn_rs,
    up_ss,
    up_fs,
    up_rs,
    base_ss,
    base_rs,
    low_ss,
    low_rs,
    ret_ss,
    rt_ss,
    ret_rs,
    out_sem,
):
    rows, width = tok_hbm.shape
    per = down_hbm.shape[0]
    depth = stores // 2
    col = depth * per
    moved = per + 2
    kv_local = up.shape[4]
    kv_whole = kv_local * tensors
    half_rows = width // HALVES
    me_s = lax.axis_index("store")
    me_t = lax.axis_index("tensor")
    z = me_s // 2
    y = me_s % 2
    low_side = z < 2
    is_mid = (z == 1) | (z == 2)
    is_end = (z == 0) | (z == 3)
    across = 3 - z
    inner = jnp.where(low_side, 1, 2)
    outer = jnp.where(low_side, 0, 3)
    z_next = jnp.where(is_mid, across, inner)
    first = jnp.where(is_mid, per, 0)

    def remote(src, dst, ss, rs, store, tensor):
        return pltpu.make_async_remote_copy(
            src_ref=src, dst_ref=dst, send_sem=ss, recv_sem=rs,
            device_id={"store": store, "tensor": tensor}, device_id_type=MESH,
        )

    def to_tensor(step):
        return (me_t + step) % tensors

    mate = me_t // 2 * 2 + 1 - me_t % 2
    far = (me_t + 2) % tensors
    far_mate = (mate + 2) % tensors
    beside = z * 2 + 1 - y

    def part_of(h):
        return pl.ds(h * half_rows, half_rows)

    tile = 128
    tok_loads = [
        pltpu.make_async_copy(
            tok_hbm.at[pl.ds(i * tile, tile)], g.at[pl.ds(i * tile, tile)], tl_sem.at[i]
        )
        for i in range(rows // tile)
    ]
    for load in tok_loads:
        load.start()
    wt = w3.shape[1]
    w_loads = [
        pltpu.make_async_copy(w_hbm.at[pl.ds(i * wt, wt)], w3.at[i % 2], w_sem.at[i % 2])
        for i in range(width // wt)
    ]
    own_loads = [
        pltpu.make_async_copy(down_hbm.at[l], down.at[first + l], ld_sem.at[l]) for l in range(per)
    ]
    up_load = pltpu.make_async_copy(up_hbm, up.at[first // per], lu_sem.at[0])

    barrier = pltpu.get_barrier_semaphore()

    def greet(store, tensor):
        pl.semaphore_signal(
            barrier, inc=1, device_id={"store": store, "tensor": tensor}, device_id_type=MESH
        )

    for step in range(1, tensors):
        greet(me_s, to_tensor(step))
    greet(beside, me_t)

    @pl.when(is_mid)
    def _():
        greet(across * 2 + y, me_t)
        for side in range(2):
            greet(outer * 2 + side, me_t)

    @pl.when(is_end)
    def _():
        for side in range(2):
            greet(inner * 2 + side, me_t)


    @pl.when(is_mid)
    def _():
        pl.semaphore_wait(barrier, tensors + 3)

    @pl.when(is_end)
    def _():
        pl.semaphore_wait(barrier, tensors + 2)


    def own_send(l, h):
        k = jnp.where(is_mid, 2 * per + l, l)
        return remote(
            down_hbm.at[l, part_of(h)], down.at[k, part_of(h)], dn_ss.at[l, h], dn_rs.at[k, h],
            z_next * 2 + y, me_t,
        )

    def up_send():
        return remote(up_hbm, up.at[0], up_ss.at[0], up_rs.at[0], z_next * 2 + y, me_t)

    def up_part(n):
        part = pl.ds(n, 1) if n < moved - per else pl.ds(n, per - n)
        return remote(
            up_hbm.at[part], up.at[2, part], up_ss.at[1 + n], up_rs.at[depth + n],
            across * 2 + y, me_t,
        )

    def forward(k, h):
        if k < per:
            to, at = across, k + 3 * per
        else:
            to, at = outer, k
        return remote(
            down.at[k, part_of(h)], down.at[at, part_of(h)], dn_fs.at[k, h], dn_rs.at[at, h],
            to * 2 + y, me_t,
        )

    def up_forward(q):
        to, at = (across, 3) if q == 0 else (outer, q)
        src, dst = up.at[q], up.at[at]
        if q == 2:
            part = pl.ds(moved - per, 2 * per - moved)
            src, dst = up.at[q, part], up.at[at, part]
        return remote(src, dst, up_fs.at[q], up_rs.at[at], to * 2 + y, me_t)

    def arrived(k, h):
        return remote(
            down.at[k, part_of(h)], down.at[k, part_of(h)], dn_fs.at[k, h], dn_rs.at[k, h],
            z_next * 2 + y, me_t,
        )

    def up_arrived(q):
        return remote(up.at[q], up.at[q], up_fs.at[q], up_rs.at[q], z_next * 2 + y, me_t)

    forwarded = [k for k in range(col) if not per <= k < per + moved]

    @pl.when(is_mid)
    def _():
        up_part(2).start()
        for l in (2, 3):
            for h in range(HALVES):
                own_send(l, h).start()

    @pl.when(is_end)
    def _():
        up_send().start()
        for h in range(HALVES):
            own_send(0, h).start()

    w_loads[0].start()
    w_loads[1].start()
    for load in own_loads:
        load.start()
    up_load.start()

    adapters = slots.shape[0]
    named = jnp.where(
        lax.broadcasted_iota(jnp.int32, (adapters, rows), 0) == ids[...], 1.0, 0.0
    )
    earlier = jnp.where(
        lax.broadcasted_iota(jnp.int32, (rows, rows), 0)
        < lax.broadcasted_iota(jnp.int32, (rows, rows), 1),
        1.0,
        0.0,
    ).astype(jnp.bfloat16)
    counts = jnp.dot(named.astype(jnp.bfloat16), earlier, preferred_element_type=jnp.float32)
    rank = jnp.sum(named * counts, axis=0, keepdims=True).astype(jnp.int32)
    slot = jnp.zeros((1, rows), jnp.int32)
    for a in range(adapters):
        slot = jnp.where(ids[...] == a, slots[a], slot)
    owner = slot // per
    plane = owner // 2
    place = jnp.where(low_side, plane, depth - 1 - plane) * per + slot % per
    other = jnp.where(owner % 2 == y, 0, col)
    trow[...] = (other + place) * cap + rank

    def scale(i, _):
        at = pl.ds(pl.multiple_of(i * tile, tile), tile)
        pltpu.make_async_copy(tok_hbm.at[at], g.at[at], tl_sem.at[i]).wait()
        x = g[at, :].astype(jnp.float32)
        g[at, :] = (x * gain[...]).astype(jnp.bfloat16)
        total = x[:, 0:128] * x[:, 0:128]
        for lane in range(1, width // 128):
            part = x[:, lane * 128 : (lane + 1) * 128]
            total = total + part * part
        sq_out[:, at] = jnp.broadcast_to(jnp.sum(total.T, axis=0, keepdims=True), (8, tile))
        return 0

    lax.fori_loop(0, rows // tile, scale, 0)

    sq_copies = [
        remote(sq_out, sq_in.at[m - 1], sq_ss.at[m - 1], sq_rs.at[m - 1], me_s, to_tensor(m))
        for m in range(1, tensors)
    ]
    for copy in sq_copies:
        copy.start()

    chunk = 512
    batch = col // 2

    def pick(group, store):
        places = lax.broadcasted_iota(jnp.int32, (batch * cap, rows), 0) + group * cap
        choose = jnp.where(places == trow[...], 1.0, 0.0).astype(jnp.bfloat16)

        def part(i, _):
            at = pl.ds(pl.multiple_of(i * chunk, chunk), chunk)
            r = jnp.dot(choose, g[:, at], preferred_element_type=jnp.float32)
            store(at, r.astype(jnp.bfloat16).reshape(batch, cap, chunk))
            return 0

        lax.fori_loop(0, width // chunk, part, 0)

    def y_copy(k):
        return remote(snd.at[k], own.at[k, 1], y_ss.at[k], y_rs.at[k], beside, me_t)

    def t_copy(j):
        return remote(
            own.at[per + j], tin.at[j], t_ss.at[j], t_rs.at[j], inner * 2 + y, me_t
        )

    for b in range(2):
        def to_snd(at, r, b=b):
            snd[b * batch : (b + 1) * batch, :, at] = r

        pick(col + b * batch, to_snd)

    mid_order = [4, 5, 6, 7, 10, 0, 11, 1, 12, 13, 2, 14, 3, 9, 15, 8]
    end_order = [4, 5, 0, 1, 2, 3, 6, 10, 7, 11, 8, 9, 12, 13, 14, 15]

    @pl.when(is_mid)
    def _():
        for k in mid_order:
            y_copy(k).start()

    @pl.when(is_end)
    def _():
        for k in end_order:
            y_copy(k).start()

    for b in range(2):
        def to_own(at, r, b=b):
            own[b * batch : (b + 1) * batch, 0, :, at] = r

        pick(b * batch, to_own)

    def mid(body):
        pl.when(is_mid)(body)

    def pump(k, halves=range(HALVES)):
        def body():
            for h in halves:
                arrived(k, h).wait_recv()
                if k in forwarded:
                    forward(k, h).start()

        mid(body)

    def pump_up(q):
        def body():
            if q == 2:
                up_part(2).wait_recv()
            else:
                up_arrived(q).wait_recv()
            up_forward(q).start()

        mid(body)

    def send_on(*moves):
        def body():
            for kind, n in moves:
                if kind == "own":
                    for h in range(HALVES):
                        own_send(n, h).start()
                else:
                    y_copy(per + n).wait_recv()
                    t_copy(n).start()

        pl.when(is_end)(body)

    send_on(("moved", 0), ("own", 1))
    pump_up(2)
    pump_up(0)

    dt = 128
    two = lax.broadcasted_iota(jnp.int32, (dt, 2 * dt), 1) - 2 * lax.broadcasted_iota(
        jnp.int32, (dt, 2 * dt), 0
    )
    every = [jnp.where(two == j, 1.0, 0.0).astype(jnp.bfloat16) for j in range(2)]
    for i in range(width // wt):
        w_loads[i].wait()

        def part_kinds(n, _, i=i):
            x = w3[i % 2, pl.ds(pl.multiple_of(n * dt, dt), dt)].reshape(2 * dt, kv_whole)
            at = pl.ds(pl.multiple_of(i * wt + n * dt, dt), dt)
            for j in range(2):
                w[at, j * kv_whole : (j + 1) * kv_whole] = jnp.dot(
                    every[j], x, preferred_element_type=jnp.float32
                ).astype(jnp.bfloat16)
            return 0

        lax.fori_loop(0, wt // dt, part_kinds, 0)
        if i + 2 < width // wt:
            w_loads[i + 2].start()

    mt = 256
    base_copies = [
        remote(base_out.at[n], base_in.at[n], base_ss.at[n], base_rs.at[n], me_s, to)
        for n, to in enumerate((mate, mate, far))
    ]

    def base(target, store):
        for j in range(2):
            cols = pl.ds(pl.multiple_of(j * kv_whole + target * kv_local, kv_local), kv_local)

            def part(i, _, j=j, cols=cols):
                at = pl.ds(pl.multiple_of(i * mt, mt), mt)
                r = jnp.dot(g[at, :], w[:, cols], preferred_element_type=jnp.float32)
                store(at, slice(j * kv_local, (j + 1) * kv_local), r)
                return 0

            lax.fori_loop(0, rows // mt, part, 0)

    def base_to(n):
        def store(at, cols, r):
            base_out[n, at, cols] = r.astype(jnp.bfloat16)

        return store

    def base_sum(at, cols, r):
        base_out[2, at, cols] = (r + base_in[0, at, cols].astype(jnp.float32)).astype(jnp.bfloat16)

    def base_own(at, cols, r):
        acc[at, cols] = r + base_in[1, at, cols].astype(jnp.float32)

    half = HEAD // 2
    lane = lax.broadcasted_iota(jnp.int32, (1, HEAD), 1)
    frequency = jnp.exp(
        (lane % half).astype(jnp.float32) * (-2.0 * math.log(rope_theta) / HEAD)
    )
    sign = jnp.where(lane < half, -1.0, 1.0)

    def tables(i, _):
        at = pl.ds(pl.multiple_of(i * tile, tile), tile)
        row = lax.broadcasted_iota(jnp.int32, (tile, HEAD), 0) + (me_s * rows + i * tile)
        position = row
        end = 0
        for r in range(lengths.shape[0]):
            end = end + lengths[r]
            position = jnp.where(row >= end, row - end, position)
        angles = position.astype(jnp.float32) * frequency
        cos_t[at, :] = jnp.cos(angles)
        sin_t[at, :] = jnp.sin(angles) * sign
        tcol[at, :] = jnp.broadcast_to(trow[:, at], (tile, tile)).T
        return 0

    def low_copy(n, m):
        return remote(
            low_out.at[n], low_in.at[m - 1, n], low_ss.at[n, m - 1], low_rs.at[n, m - 1],
            me_s, to_tensor(m),
        )

    def lower_rows(n, k, x):
        r = jnp.dot(x, down[k], preferred_element_type=jnp.float32)
        low_own[n] = r
        low_out[n] = r.astype(jnp.bfloat16)
        for m in range(1, tensors):
            low_copy(n, m).start()

    def lower(k):
        y_copy(k).wait_recv()
        lower_rows(k, k, own[k].reshape(2 * cap, width))

    def lower_moved(j):
        t_copy(j).wait_recv()
        lower_rows(col + j, per + j, tin[j].reshape(2 * cap, width))

    def raised(n, k):
        total = low_own[n]
        for m in range(1, tensors):
            low_copy(n, m).wait_recv()
            total = total + low_in[m - 1, n].astype(jnp.float32)
        middle = (total * adapter_scale).astype(jnp.bfloat16)
        return [
            jnp.dot(
                middle[:, j * ADAPTER_RANK : (j + 1) * ADAPTER_RANK],
                up[k // per, k % per, j],
                preferred_element_type=jnp.float32,
            ).astype(jnp.bfloat16)
            for j in range(2)
        ]

    def ret_copy(k):
        return remote(
            ret_y.at[k], ret.at[col + k], ret_ss.at[k], ret_rs.at[col + k], beside, me_t
        )

    def moved_copy(j, cross):
        at = per + j + (col if cross else 0)
        to = outer * 2 + (1 - y if cross else y)
        return remote(ret_t.at[j, cross], ret.at[at], rt_ss.at[j, cross], ret_rs.at[at], to, me_t)

    def raise_back(k):
        for j, d in enumerate(raised(k, k)):
            cols = slice(j * kv_local, (j + 1) * kv_local)
            ret[k, :, cols] = d[:cap]
            ret_y[k, :, cols] = d[cap:]
        ret_copy(k).start()

    def raise_moved(n):
        for j, d in enumerate(raised(col + n, per + n)):
            cols = slice(j * kv_local, (j + 1) * kv_local)
            ret_t[n, 0, :, cols] = d[:cap]
            ret_t[n, 1, :, cols] = d[cap:]
        moved_copy(n, 0).start()
        moved_copy(n, 1).start()

    def lower_far(k):
        @pl.when(is_end)
        def _():
            for h in range(HALVES):
                arrived(k, h).wait_recv()

        lower(k)

    def given(at, total, spans):
        for lo, hi in spans:
            count = (hi - lo) * cap
            lanes = lax.broadcasted_iota(jnp.int32, (mt, count), 1)
            for start in (lo, col + lo):
                choose = jnp.where(lanes + start * cap == tcol[at, 0:1], 1.0, 0.0)
                total = total + jnp.dot(
                    choose.astype(jnp.bfloat16),
                    ret[start : start + hi - lo].reshape(count, 2 * kv_local),
                    preferred_element_type=jnp.float32,
                )
        return total

    def give(*spans):
        def part(i, _):
            at = pl.ds(pl.multiple_of(i * mt, mt), mt)
            acc[at, :] = given(at, acc[at, :], spans)
            return 0

        lax.fori_loop(0, rows // mt, part, 0)

    def join(i, _):
        at = pl.ds(pl.multiple_of(i * tile, tile), tile)
        square = sq_out[0:1, at]
        for m in range(tensors - 1):
            square = square + sq_in[m, 0:1, at]
        scale_row = lax.rsqrt(square / (width * tensors) + epsilon)
        scale_t[at, :] = jnp.broadcast_to(scale_row, (tile, tile)).T
        acc[at, :] = acc[at, :] + base_in[2, at, :].astype(jnp.float32)
        return 0

    def relay(l):
        @pl.when(is_mid)
        def _():
            for h in range(HALVES):
                own_send(l, h).start()

    pump(10)
    pump(0)
    base(far_mate, base_to(0))
    base_copies[0].start()
    base(mate, base_to(1))
    base_copies[1].start()
    send_on(("moved", 1), ("own", 2), ("own", 3))
    for load in own_loads:
        load.wait()
    for l in range(per):
        lower(first + l)
    pump(11)
    base_copies[0].wait_recv()
    base(far, base_sum)
    base_copies[2].start()
    base_copies[1].wait_recv()
    base(me_t, base_own)
    pump(1)

    @pl.when(is_mid)
    def _():
        up_arrived(3).wait_recv()
        up_forward(3).start()

    up_load.wait()
    for l in range(per):
        raise_back(first + l)
    lax.fori_loop(0, rows // tile, tables, 0)
    send_on(("moved", 2))
    mid(lambda: lower(0))
    lower_far(10)
    send_on(("moved", 3))

    @pl.when(is_mid)
    def _():
        lower(1)
        lower_moved(0)

    pump(12)
    lower_far(11)
    send_on(("moved", 4), ("moved", 5))
    mid(lambda: lower_moved(1))
    lower_far(12)
    pump(13, [0])
    pump(2)
    relay(1)
    pump(13, range(1, HALVES))
    lower_far(13)
    mid(lambda: lower(2))

    @pl.when(is_end)
    def _():
        up_forward(2).wait_recv()

    mid(lambda: raise_back(0))
    raise_back(10)
    for copy in sq_copies:
        copy.wait_recv()
    base_copies[2].wait_recv()
    lax.fori_loop(0, rows // tile, join, 0)
    raise_back(11)

    @pl.when(is_mid)
    def _():
        raise_back(1)
        raise_moved(0)
        raise_moved(1)

    @pl.when(is_end)
    def _():
        up_arrived(3).wait_recv()

    raise_back(12)
    pump(14)
    pump(3)
    relay(0)

    @pl.when(is_mid)
    def _():
        up_part(1).start()
        up_part(0).start()

    lower_far(14)
    mid(lambda: lower(3))
    raise_back(13)
    mid(lambda: raise_back(2))
    mid(lambda: lower_moved(2))
    raise_back(14)
    pump(9)

    @pl.when(is_mid)
    def _():
        lower(9)
        raise_back(3)
        raise_moved(2)
        lower_moved(3)

    pump(15)
    lower_far(15)

    @pl.when(is_mid)
    def _():
        raise_moved(3)
        lower_moved(5)

    last = 2 * per
    shared = [k for k in range(col) if k < per or k >= per + moved]
    for k in shared[:-1]:
        ret_copy(k).wait_recv()

    @pl.when(is_mid)
    def _():
        for k in range(per, last):
            ret_copy(k).wait_recv()

    @pl.when(is_end)
    def _():
        for j in range(per):
            for cross in range(2):
                moved_copy(j, cross).wait_recv()

    give((0, last), (last + 2, col - 1))
    raise_back(15)
    ret_copy(15).wait_recv()
    give((col - 1, col))

    @pl.when(is_mid)
    def _():
        for h in range(HALVES):
            arrived(last, h).wait_recv()
        lower(last)
        lower_moved(per)
        up_part(1).wait_recv()
        raise_moved(per + 1)
        raise_back(last + 1)
        up_part(0).wait_recv()
        raise_moved(per)
        raise_back(last)
        ret_copy(last + 1).wait_recv()
        ret_copy(last).wait_recv()

    @pl.when(is_end)
    def _():
        for j in (per + 1, per):
            for cross in range(2):
                moved_copy(j, cross).wait_recv()

    def finish(i, _):
        at = pl.ds(i * mt, mt)
        total = given(at, acc[at, :], ((last, last + 2),)) * scale_t[at, 0:1]
        c = cos_t[at, :]
        s = sin_t[at, :]
        for head in range(kv_local // HEAD):
            x = total[:, head * HEAD : (head + 1) * HEAD]
            r = x * c + pltpu.roll(x, HEAD // 2, 1) * s
            out[at, head * HEAD : (head + 1) * HEAD] = r.astype(jnp.bfloat16)
        out[at, kv_local:] = total[:, kv_local:].astype(jnp.bfloat16)
        pltpu.make_async_copy(out.at[at], out_hbm.at[at], out_sem.at[i]).start()
        return 0

    for i in range(rows // mt):
        finish(i, 0)

    for copy in sq_copies + base_copies:
        copy.wait_send()
    for l in range(per):
        for h in range(HALVES):
            own_send(l, h).wait_send()
    for k in range(col):
        y_copy(k).wait_send()

    def sent(k):
        ret_copy(k).wait_send()
        for m in range(1, tensors):
            low_copy(k, m).wait_send()

    for k in shared:
        sent(k)

    @pl.when(is_mid)
    def _():
        for k in forwarded:
            for h in range(HALVES):
                forward(k, h).wait_send()
        for q in (0, 2, 3):
            up_forward(q).wait_send()
        for n in range(3):
            up_part(n).wait_send()
        for k in range(per, per + moved):
            sent(k)
        for j in range(moved):
            for m in range(1, tensors):
                low_copy(col + j, m).wait_send()
            for cross in range(2):
                moved_copy(j, cross).wait_send()

    for i in range(rows // mt):
        at = pl.ds(i * mt, mt)
        pltpu.make_async_copy(out.at[at], out_hbm.at[at], out_sem.at[i]).wait()

    @pl.when(is_end)
    def _():
        up_send().wait_send()
        for j in range(moved):
            t_copy(j).wait_send()


def fused(
    tokens,
    norm_gain,
    kv_weight,
    adapter_down,
    adapter_up,
    token_adapters,
    adapter_slot,
    request_lengths,
):
    rows, width = tokens.shape
    capacity = max(2, 5 * rows // (4 * adapter_slot.shape[0]))
    cap = -(-capacity // 8) * 8
    stores = lax.axis_size("store")
    tensors = lax.axis_size("tensor")
    per, _, _, kv_local = adapter_up.shape
    depth = stores // 2
    col = depth * per
    moved = per + 2
    ranks = adapter_down.shape[2]
    vmem = pl.BlockSpec(memory_space=pltpu.VMEM)
    smem = pl.BlockSpec(memory_space=pltpu.SMEM)
    hbm = pl.BlockSpec(memory_space=pl.ANY)
    f32, bf16 = jnp.float32, jnp.bfloat16
    dma = pltpu.SemaphoreType.DMA
    both = pl.pallas_call(
        functools.partial(fused_kernel, stores, tensors, cap),
        out_shape=jax.ShapeDtypeStruct((rows, 2 * kv_local), bf16),
        in_specs=[vmem] * 2 + [smem] * 2 + [hbm] * 4,
        out_specs=hbm,
        scratch_shapes=[
            pltpu.VMEM((rows, 2 * kv_local), bf16),
            pltpu.VMEM((1, rows), jnp.int32),
            pltpu.VMEM((rows, 128), jnp.int32),
            pltpu.VMEM((rows, HEAD), f32),
            pltpu.VMEM((rows, HEAD), f32),
            pltpu.VMEM((rows, 128), f32),
            pltpu.VMEM((rows, width), bf16),
            pltpu.VMEM((2, 256, 2, kv_local * tensors), bf16),
            pltpu.VMEM((width, 2 * kv_local * tensors), bf16),
            pltpu.VMEM((col, width, ranks), bf16),
            pltpu.VMEM((depth, per, 2, ADAPTER_RANK, kv_local), bf16),
            pltpu.VMEM((col, 2, cap, width), bf16),
            pltpu.VMEM((col, cap, width), bf16),
            pltpu.VMEM((moved, 2, cap, width), bf16),
            pltpu.VMEM((8, rows), f32),
            pltpu.VMEM((tensors - 1, 8, rows), f32),
            pltpu.VMEM((rows, 2 * kv_local), f32),
            pltpu.VMEM((3, rows, 2 * kv_local), bf16),
            pltpu.VMEM((3, rows, 2 * kv_local), bf16),
            pltpu.VMEM((col + moved, 2 * cap, ranks), f32),
            pltpu.VMEM((col + moved, 2 * cap, ranks), bf16),
            pltpu.VMEM((tensors - 1, col + moved, 2 * cap, ranks), bf16),
            pltpu.VMEM((2 * col, cap, 2 * kv_local), bf16),
            pltpu.VMEM((col, cap, 2 * kv_local), bf16),
            pltpu.VMEM((moved, 2, cap, 2 * kv_local), bf16),
            dma((rows // 128,)),
            dma((2,)),
            dma((per,)),
            dma((1,)),
            dma((tensors - 1,)),
            dma((tensors - 1,)),
            dma((col,)),
            dma((col,)),
            dma((moved,)),
            dma((moved,)),
            dma((per, HALVES)),
            dma((col, HALVES)),
            dma((col, HALVES)),
            dma((2 + depth,)),
            dma((depth,)),
            dma((depth + 3,)),
            dma((3,)),
            dma((3,)),
            dma((col + moved, tensors - 1)),
            dma((col + moved, tensors - 1)),
            dma((col,)),
            dma((moved, 2)),
            dma((2 * col,)),
            dma((rows // 256,)),
        ],
        compiler_params=pltpu.CompilerParams(
            collective_id=0, has_side_effects=True, vmem_limit_bytes=63 * 1024 * 1024
        ),
    )(
        norm_gain[None, :],
        token_adapters.reshape(1, rows),
        adapter_slot,
        request_lengths,
        tokens,
        adapter_up,
        kv_weight,
        adapter_down,
    )
    return both[:, :kv_local], both[:, kv_local:]


def local(
    tokens,
    norm_gain,
    kv_weight,
    adapter_down,
    adapter_up,
    token_adapters,
    adapter_slot,
    request_lengths,
):
    row_count = tokens.shape[0]
    local_width = tokens.shape[1]
    adapter_total = adapter_slot.shape[0]
    capacity = max(2, 5 * row_count // (4 * adapter_total))
    store_size = lax.axis_size("store")
    per_owner = adapter_down.shape[0]
    kv_local = adapter_up.shape[3]
    widened = tokens.astype(jnp.float32)
    squares = lax.psum(jnp.sum(widened * widened, axis=1), "tensor")
    normed = (widened * lax.rsqrt(squares / D + epsilon)[:, None] * norm_gain[None, :]).astype(
        jnp.bfloat16
    )
    targets = place_rows(token_adapters[:, 0], adapter_slot, capacity)
    send_rows = (
        jnp.zeros((adapter_total * capacity, local_width), jnp.bfloat16).at[targets].set(normed)
    )
    send_rows = send_rows.reshape(store_size, per_owner, capacity, local_width)
    down_projected = jnp.einsum(
        "slcd,ldr->slcr",
        lax.all_to_all(send_rows, "store", split_axis=0, concat_axis=0, tiled=True),
        adapter_down,
        preferred_element_type=jnp.float32,
    )
    rank_total_sum = lax.psum(down_projected, "tensor")
    rank_activation = (rank_total_sum * adapter_scale).astype(jnp.bfloat16)
    split_rank = rank_activation.reshape(rank_activation.shape[:3] + (2, ADAPTER_RANK))
    update_rows = jnp.einsum(
        "slcjr,ljrk->slcjk", split_rank, adapter_up, preferred_element_type=jnp.float32
    )
    back_rows = update_rows.astype(jnp.bfloat16).reshape(
        rank_activation.shape[:3] + (2 * kv_local,)
    )
    returned = lax.all_to_all(back_rows, "store", split_axis=0, concat_axis=0, tiled=True)
    delta_rows = returned.reshape(adapter_total * capacity, 2, kv_local)[targets]
    partial_value = jnp.einsum("td,djk->tjk", normed, kv_weight, preferred_element_type=jnp.float32)
    base_part = lax.psum_scatter(partial_value, "tensor", scatter_dimension=2, tiled=True)
    combined = base_part + delta_rows.astype(jnp.float32)
    positions = positions_of(lax.axis_index("store") * row_count, row_count, request_lengths)
    new_keys = rotate(combined[:, 0, :], positions).astype(jnp.bfloat16)
    new_values = combined[:, 1, :].astype(jnp.bfloat16)
    return (new_keys, new_values)


def solution(mesh):
    small = mesh.shape["store"] == 8 and mesh.shape["tensor"] == 4
    return jax.shard_map(
        fused if small else local,
        mesh=mesh,
        in_specs=(
            P("store", "tensor"),
            P("tensor"),
            P("tensor", None, None),
            P("store", "tensor", None),
            P("store", None, None, "tensor"),
            P("store", None),
            P(),
            P(),
        ),
        out_specs=(P("store", "tensor"), P("store", "tensor")),
        check_vma=False,
    )
```

```python
import functools
import math

import jax
import jax.numpy as jnp
from jax import lax
from jax.experimental import pallas as pl
from jax.experimental.pallas import tpu as pltpu
from jax.sharding import PartitionSpec as P

D = 8192
HEAD = 128
ADAPTER_RANK = 64


epsilon = 1e-05
adapter_scale = 2.0
rope_theta = 500000.0


def place_rows(adapter_ids, adapter_slot, capacity):
    catalog = jnp.arange(adapter_slot.shape[0], dtype=jnp.int32)
    slot_rows = jnp.sum(
        jnp.where(adapter_ids[:, None] == catalog[None, :], adapter_slot[None, :], 0), axis=1
    )
    row_order = jnp.arange(adapter_ids.shape[0], dtype=jnp.int32)
    same_earlier = (adapter_ids[:, None] == adapter_ids[None, :]) & (
        row_order[None, :] < row_order[:, None]
    )
    rank_rows = jnp.sum(same_earlier.astype(jnp.int32), axis=1)
    return slot_rows * capacity + rank_rows


def positions_of(first_row, row_count, lengths):
    global_rows = first_row + jnp.arange(row_count, dtype=jnp.int32)
    request_ends = jnp.cumsum(lengths)
    preceding = jnp.sum(
        jnp.where(request_ends[None, :] <= global_rows[:, None], lengths[None, :], 0), axis=1
    )
    return global_rows - preceding


def rotate(states, positions):
    per_head = states.reshape(states.shape[0], -1, HEAD)
    half_size = HEAD // 2
    frequency = jnp.exp(
        jnp.arange(half_size, dtype=jnp.float32) * (-2.0 * math.log(rope_theta) / HEAD)
    )
    angles = positions.astype(jnp.float32)[:, None] * frequency[None, :]
    cos_part = jnp.concatenate([jnp.cos(angles), jnp.cos(angles)], axis=1)[:, None, :]
    sin_part = jnp.concatenate([jnp.sin(angles), jnp.sin(angles)], axis=1)[:, None, :]
    low_half = per_head[..., :half_size]
    high_half = per_head[..., half_size:]
    turned = jnp.concatenate([-high_half, low_half], axis=-1)
    return (per_head * cos_part + turned * sin_part).reshape(states.shape)


MESH = pl.DeviceIdType.MESH


HALVES = 2


def fused_kernel(
    stores,
    tensors,
    cap,
    gain,
    ids,
    slots,
    lengths,
    tok_hbm,
    up_hbm,
    w_hbm,
    down_hbm,
    out_hbm,
    out,
    trow,
    tcol,
    cos_t,
    sin_t,
    scale_t,
    g,
    w3,
    w,
    down,
    up,
    own,
    snd,
    tin,
    sq_out,
    sq_in,
    acc,
    base_out,
    base_in,
    low_own,
    low_out,
    low_in,
    ret,
    ret_y,
    ret_t,
    tl_sem,
    w_sem,
    ld_sem,
    lu_sem,
    sq_ss,
    sq_rs,
    y_ss,
    y_rs,
    t_ss,
    t_rs,
    dn_ss,
    dn_fs,
    dn_rs,
    up_ss,
    up_fs,
    up_rs,
    base_ss,
    base_rs,
    low_ss,
    low_rs,
    ret_ss,
    rt_ss,
    ret_rs,
    out_sem,
    ready,
):
    rows, width = tok_hbm.shape
    per = down_hbm.shape[0]
    depth = stores // 2
    col = depth * per
    moved = per + 2
    kv_local = up.shape[4]
    kv_whole = kv_local * tensors
    half_rows = width // HALVES
    me_s = lax.axis_index("store")
    me_t = lax.axis_index("tensor")
    z = me_s // 2
    y = me_s % 2
    low_side = z < 2
    is_mid = (z == 1) | (z == 2)
    is_end = (z == 0) | (z == 3)
    across = 3 - z
    inner = jnp.where(low_side, 1, 2)
    outer = jnp.where(low_side, 0, 3)
    z_next = jnp.where(is_mid, across, inner)
    first = jnp.where(is_mid, per, 0)

    def remote(src, dst, ss, rs, store, tensor):
        return pltpu.make_async_remote_copy(
            src_ref=src, dst_ref=dst, send_sem=ss, recv_sem=rs,
            device_id={"store": store, "tensor": tensor}, device_id_type=MESH,
        )

    def to_tensor(step):
        return (me_t + step) % tensors

    mate = me_t // 2 * 2 + 1 - me_t % 2
    far = (me_t + 2) % tensors
    far_mate = (mate + 2) % tensors
    beside = z * 2 + 1 - y

    def part_of(h):
        return pl.ds(h * half_rows, half_rows)

    tile = 128
    tok_loads = [
        pltpu.make_async_copy(
            tok_hbm.at[pl.ds(i * tile, tile)], g.at[pl.ds(i * tile, tile)], tl_sem.at[i]
        )
        for i in range(rows // tile)
    ]
    for load in tok_loads:
        load.start()
    wt = w3.shape[1]
    w_loads = [
        pltpu.make_async_copy(w_hbm.at[pl.ds(i * wt, wt)], w3.at[i % 2], w_sem.at[i % 2])
        for i in range(width // wt)
    ]
    own_loads = [
        pltpu.make_async_copy(down_hbm.at[l], down.at[first + l], ld_sem.at[l]) for l in range(per)
    ]
    up_load = pltpu.make_async_copy(up_hbm, up.at[first // per], lu_sem.at[0])

    barrier = pltpu.get_barrier_semaphore()

    def greet(store, tensor):
        pl.semaphore_signal(
            barrier, inc=1, device_id={"store": store, "tensor": tensor}, device_id_type=MESH
        )

    for step in range(1, tensors):
        greet(me_s, to_tensor(step))
    greet(beside, me_t)

    @pl.when(is_mid)
    def _():
        greet(across * 2 + y, me_t)
        for side in range(2):
            greet(outer * 2 + side, me_t)


    @pl.when(is_mid)
    def _():
        pl.semaphore_wait(barrier, tensors + 1)

    @pl.when(is_end)
    def _():
        pl.semaphore_wait(barrier, tensors + 2)
        for side in range(2):
            pl.semaphore_signal(
                ready, inc=1, device_id={"store": inner * 2 + side, "tensor": me_t},
                device_id_type=MESH,
            )


    def own_send(l, h):
        k = jnp.where(is_mid, 2 * per + l, l)
        return remote(
            down_hbm.at[l, part_of(h)], down.at[k, part_of(h)], dn_ss.at[l, h], dn_rs.at[k, h],
            z_next * 2 + y, me_t,
        )

    def up_send():
        return remote(up_hbm, up.at[0], up_ss.at[0], up_rs.at[0], z_next * 2 + y, me_t)

    def up_part(n):
        part = pl.ds(n, 1) if n < moved - per else pl.ds(n, per - n)
        return remote(
            up_hbm.at[part], up.at[2, part], up_ss.at[1 + n], up_rs.at[depth + n],
            across * 2 + y, me_t,
        )

    def forward(k, h):
        if k < per:
            to, at = across, k + 3 * per
        else:
            to, at = outer, k
        return remote(
            down.at[k, part_of(h)], down.at[at, part_of(h)], dn_fs.at[k, h], dn_rs.at[at, h],
            to * 2 + y, me_t,
        )

    def up_forward(q):
        to, at = (across, 3) if q == 0 else (outer, q)
        src, dst = up.at[q], up.at[at]
        if q == 2:
            part = pl.ds(moved - per, 2 * per - moved)
            src, dst = up.at[q, part], up.at[at, part]
        return remote(src, dst, up_fs.at[q], up_rs.at[at], to * 2 + y, me_t)

    def arrived(k, h):
        return remote(
            down.at[k, part_of(h)], down.at[k, part_of(h)], dn_fs.at[k, h], dn_rs.at[k, h],
            z_next * 2 + y, me_t,
        )

    def up_arrived(q):
        return remote(up.at[q], up.at[q], up_fs.at[q], up_rs.at[q], z_next * 2 + y, me_t)

    forwarded = [k for k in range(col) if not per <= k < per + moved]

    @pl.when(is_mid)
    def _():
        up_part(2).start()
        for l in (2, 3):
            for h in range(HALVES):
                own_send(l, h).start()

    @pl.when(is_end)
    def _():
        up_send().start()
        for h in range(HALVES):
            own_send(0, h).start()

    w_loads[0].start()
    w_loads[1].start()
    for load in own_loads:
        load.start()
    up_load.start()

    adapters = slots.shape[0]
    named = jnp.where(
        lax.broadcasted_iota(jnp.int32, (adapters, rows), 0) == ids[...], 1.0, 0.0
    )
    earlier = jnp.where(
        lax.broadcasted_iota(jnp.int32, (rows, rows), 0)
        < lax.broadcasted_iota(jnp.int32, (rows, rows), 1),
        1.0,
        0.0,
    ).astype(jnp.bfloat16)
    counts = jnp.dot(named.astype(jnp.bfloat16), earlier, preferred_element_type=jnp.float32)
    rank = jnp.sum(named * counts, axis=0, keepdims=True).astype(jnp.int32)
    slot = jnp.zeros((1, rows), jnp.int32)
    for a in range(adapters):
        slot = jnp.where(ids[...] == a, slots[a], slot)
    owner = slot // per
    plane = owner // 2
    place = jnp.where(low_side, plane, depth - 1 - plane) * per + slot % per
    other = jnp.where(owner % 2 == y, 0, col)
    trow[...] = (other + place) * cap + rank

    def scale(i, _):
        at = pl.ds(pl.multiple_of(i * tile, tile), tile)
        pltpu.make_async_copy(tok_hbm.at[at], g.at[at], tl_sem.at[i]).wait()
        x = g[at, :].astype(jnp.float32)
        g[at, :] = (x * gain[...]).astype(jnp.bfloat16)
        total = x[:, 0:128] * x[:, 0:128]
        for lane in range(1, width // 128):
            part = x[:, lane * 128 : (lane + 1) * 128]
            total = total + part * part
        sq_out[:, at] = jnp.broadcast_to(jnp.sum(total.T, axis=0, keepdims=True), (8, tile))
        return 0

    lax.fori_loop(0, rows // tile, scale, 0)

    sq_copies = [
        remote(sq_out, sq_in.at[m - 1], sq_ss.at[m - 1], sq_rs.at[m - 1], me_s, to_tensor(m))
        for m in range(1, tensors)
    ]
    for copy in sq_copies:
        copy.start()

    chunk = 512
    batch = col // 2

    def pick(group, store):
        places = lax.broadcasted_iota(jnp.int32, (batch * cap, rows), 0) + group * cap
        choose = jnp.where(places == trow[...], 1.0, 0.0).astype(jnp.bfloat16)

        def part(i, _):
            at = pl.ds(pl.multiple_of(i * chunk, chunk), chunk)
            r = jnp.dot(choose, g[:, at], preferred_element_type=jnp.float32)
            store(at, r.astype(jnp.bfloat16).reshape(batch, cap, chunk))
            return 0

        lax.fori_loop(0, width // chunk, part, 0)

    def y_copy(k):
        return remote(snd.at[k], own.at[k, 1], y_ss.at[k], y_rs.at[k], beside, me_t)

    def t_copy(j):
        return remote(
            own.at[per + j], tin.at[j], t_ss.at[j], t_rs.at[j], inner * 2 + y, me_t
        )

    for b in range(2):
        def to_snd(at, r, b=b):
            snd[b * batch : (b + 1) * batch, :, at] = r

        pick(col + b * batch, to_snd)

    mid_order = [4, 5, 6, 7, 10, 0, 11, 1, 12, 13, 2, 14, 3, 9, 15, 8]
    end_order = [4, 5, 0, 1, 2, 3, 6, 10, 7, 11, 8, 9, 12, 13, 14, 15]

    @pl.when(is_mid)
    def _():
        for k in mid_order:
            y_copy(k).start()

    @pl.when(is_end)
    def _():
        for k in end_order:
            y_copy(k).start()

    for b in range(2):
        def to_own(at, r, b=b):
            own[b * batch : (b + 1) * batch, 0, :, at] = r

        pick(b * batch, to_own)

    def mid(body):
        pl.when(is_mid)(body)

    def pump(k, halves=range(HALVES)):
        def body():
            for h in halves:
                arrived(k, h).wait_recv()
                if k in forwarded:
                    forward(k, h).start()

        mid(body)

    def pump_up(q):
        def body():
            if q == 2:
                up_part(2).wait_recv()
            else:
                up_arrived(q).wait_recv()
            up_forward(q).start()

        mid(body)

    def send_on(*moves):
        def body():
            for kind, n in moves:
                if kind == "own":
                    for h in range(HALVES):
                        own_send(n, h).start()
                else:
                    y_copy(per + n).wait_recv()
                    t_copy(n).start()

        pl.when(is_end)(body)

    send_on(("moved", 0), ("own", 1))
    @pl.when(is_mid)
    def _():
        pl.semaphore_wait(ready, 2)

    pump_up(2)
    pump_up(0)

    dt = 128
    two = lax.broadcasted_iota(jnp.int32, (dt, 2 * dt), 1) - 2 * lax.broadcasted_iota(
        jnp.int32, (dt, 2 * dt), 0
    )
    every = [jnp.where(two == j, 1.0, 0.0).astype(jnp.bfloat16) for j in range(2)]
    for i in range(width // wt):
        w_loads[i].wait()

        def part_kinds(n, _, i=i):
            x = w3[i % 2, pl.ds(pl.multiple_of(n * dt, dt), dt)].reshape(2 * dt, kv_whole)
            at = pl.ds(pl.multiple_of(i * wt + n * dt, dt), dt)
            for j in range(2):
                w[at, j * kv_whole : (j + 1) * kv_whole] = jnp.dot(
                    every[j], x, preferred_element_type=jnp.float32
                ).astype(jnp.bfloat16)
            return 0

        lax.fori_loop(0, wt // dt, part_kinds, 0)
        if i + 2 < width // wt:
            w_loads[i + 2].start()

    mt = 256
    base_copies = [
        remote(base_out.at[n], base_in.at[n], base_ss.at[n], base_rs.at[n], me_s, to)
        for n, to in enumerate((mate, mate, far))
    ]

    def base(target, store):
        for j in range(2):
            cols = pl.ds(pl.multiple_of(j * kv_whole + target * kv_local, kv_local), kv_local)

            def part(i, _, j=j, cols=cols):
                at = pl.ds(pl.multiple_of(i * mt, mt), mt)
                r = jnp.dot(g[at, :], w[:, cols], preferred_element_type=jnp.float32)
                store(at, slice(j * kv_local, (j + 1) * kv_local), r)
                return 0

            lax.fori_loop(0, rows // mt, part, 0)

    def base_to(n):
        def store(at, cols, r):
            base_out[n, at, cols] = r.astype(jnp.bfloat16)

        return store

    def base_sum(at, cols, r):
        base_out[2, at, cols] = (r + base_in[0, at, cols].astype(jnp.float32)).astype(jnp.bfloat16)

    def base_own(at, cols, r):
        acc[at, cols] = r + base_in[1, at, cols].astype(jnp.float32)

    half = HEAD // 2
    lane = lax.broadcasted_iota(jnp.int32, (1, HEAD), 1)
    frequency = jnp.exp(
        (lane % half).astype(jnp.float32) * (-2.0 * math.log(rope_theta) / HEAD)
    )
    sign = jnp.where(lane < half, -1.0, 1.0)

    def tables(i, _):
        at = pl.ds(pl.multiple_of(i * tile, tile), tile)
        row = lax.broadcasted_iota(jnp.int32, (tile, HEAD), 0) + (me_s * rows + i * tile)
        position = row
        end = 0
        for r in range(lengths.shape[0]):
            end = end + lengths[r]
            position = jnp.where(row >= end, row - end, position)
        angles = position.astype(jnp.float32) * frequency
        cos_t[at, :] = jnp.cos(angles)
        sin_t[at, :] = jnp.sin(angles) * sign
        tcol[at, :] = jnp.broadcast_to(trow[:, at], (tile, tile)).T
        return 0

    def low_copy(n, m):
        return remote(
            low_out.at[n], low_in.at[m - 1, n], low_ss.at[n, m - 1], low_rs.at[n, m - 1],
            me_s, to_tensor(m),
        )

    def lower_rows(n, k, x):
        r = jnp.dot(x, down[k], preferred_element_type=jnp.float32)
        low_own[n] = r
        low_out[n] = r.astype(jnp.bfloat16)
        for m in range(1, tensors):
            low_copy(n, m).start()

    def lower(k):
        y_copy(k).wait_recv()
        lower_rows(k, k, own[k].reshape(2 * cap, width))

    def lower_moved(j):
        t_copy(j).wait_recv()
        lower_rows(col + j, per + j, tin[j].reshape(2 * cap, width))

    def raised(n, k):
        total = low_own[n]
        for m in range(1, tensors):
            low_copy(n, m).wait_recv()
            total = total + low_in[m - 1, n].astype(jnp.float32)
        middle = (total * adapter_scale).astype(jnp.bfloat16)
        return [
            jnp.dot(
                middle[:, j * ADAPTER_RANK : (j + 1) * ADAPTER_RANK],
                up[k // per, k % per, j],
                preferred_element_type=jnp.float32,
            ).astype(jnp.bfloat16)
            for j in range(2)
        ]

    def ret_copy(k):
        return remote(
            ret_y.at[k], ret.at[col + k], ret_ss.at[k], ret_rs.at[col + k], beside, me_t
        )

    def moved_copy(j, cross):
        at = per + j + (col if cross else 0)
        to = outer * 2 + (1 - y if cross else y)
        return remote(ret_t.at[j, cross], ret.at[at], rt_ss.at[j, cross], ret_rs.at[at], to, me_t)

    def raise_back(k):
        for j, d in enumerate(raised(k, k)):
            cols = slice(j * kv_local, (j + 1) * kv_local)
            ret[k, :, cols] = d[:cap]
            ret_y[k, :, cols] = d[cap:]
        ret_copy(k).start()

    def raise_moved(n):
        for j, d in enumerate(raised(col + n, per + n)):
            cols = slice(j * kv_local, (j + 1) * kv_local)
            ret_t[n, 0, :, cols] = d[:cap]
            ret_t[n, 1, :, cols] = d[cap:]
        moved_copy(n, 0).start()
        moved_copy(n, 1).start()

    def lower_far(k):
        @pl.when(is_end)
        def _():
            for h in range(HALVES):
                arrived(k, h).wait_recv()

        lower(k)

    def given(at, total, spans):
        for lo, hi in spans:
            count = (hi - lo) * cap
            lanes = lax.broadcasted_iota(jnp.int32, (mt, count), 1)
            for start in (lo, col + lo):
                choose = jnp.where(lanes + start * cap == tcol[at, 0:1], 1.0, 0.0)
                total = total + jnp.dot(
                    choose.astype(jnp.bfloat16),
                    ret[start : start + hi - lo].reshape(count, 2 * kv_local),
                    preferred_element_type=jnp.float32,
                )
        return total

    def give(*spans):
        def part(i, _):
            at = pl.ds(pl.multiple_of(i * mt, mt), mt)
            acc[at, :] = given(at, acc[at, :], spans)
            return 0

        lax.fori_loop(0, rows // mt, part, 0)

    def join(i, _):
        at = pl.ds(pl.multiple_of(i * tile, tile), tile)
        square = sq_out[0:1, at]
        for m in range(tensors - 1):
            square = square + sq_in[m, 0:1, at]
        scale_row = lax.rsqrt(square / (width * tensors) + epsilon)
        scale_t[at, :] = jnp.broadcast_to(scale_row, (tile, tile)).T
        acc[at, :] = acc[at, :] + base_in[2, at, :].astype(jnp.float32)
        return 0

    def relay(l):
        @pl.when(is_mid)
        def _():
            for h in range(HALVES):
                own_send(l, h).start()

    pump(10)
    pump(0)
    base(far_mate, base_to(0))
    base_copies[0].start()
    base(mate, base_to(1))
    base_copies[1].start()
    send_on(("moved", 1), ("own", 2), ("own", 3))
    for load in own_loads:
        load.wait()
    for l in range(per):
        lower(first + l)
    pump(11)
    base_copies[0].wait_recv()
    base(far, base_sum)
    base_copies[2].start()
    base_copies[1].wait_recv()
    base(me_t, base_own)
    pump(1)

    @pl.when(is_mid)
    def _():
        up_arrived(3).wait_recv()
        up_forward(3).start()

    up_load.wait()
    for l in range(per):
        raise_back(first + l)
    lax.fori_loop(0, rows // tile, tables, 0)
    send_on(("moved", 2))
    mid(lambda: lower(0))
    lower_far(10)
    send_on(("moved", 3))

    @pl.when(is_mid)
    def _():
        lower(1)
        lower_moved(0)

    pump(12)
    lower_far(11)
    send_on(("moved", 4), ("moved", 5))
    mid(lambda: lower_moved(1))
    lower_far(12)
    pump(13, [0])
    pump(2)
    relay(1)
    pump(13, range(1, HALVES))
    lower_far(13)
    mid(lambda: lower(2))

    @pl.when(is_end)
    def _():
        up_forward(2).wait_recv()

    mid(lambda: raise_back(0))
    raise_back(10)
    for copy in sq_copies:
        copy.wait_recv()
    base_copies[2].wait_recv()
    lax.fori_loop(0, rows // tile, join, 0)
    raise_back(11)

    @pl.when(is_mid)
    def _():
        raise_back(1)
        raise_moved(0)
        raise_moved(1)

    @pl.when(is_end)
    def _():
        up_arrived(3).wait_recv()

    raise_back(12)
    pump(14)
    pump(3)
    relay(0)

    @pl.when(is_mid)
    def _():
        up_part(1).start()
        up_part(0).start()

    lower_far(14)
    mid(lambda: lower(3))
    raise_back(13)
    mid(lambda: raise_back(2))
    mid(lambda: lower_moved(2))
    raise_back(14)
    pump(9)

    @pl.when(is_mid)
    def _():
        lower(9)
        raise_back(3)
        raise_moved(2)
        lower_moved(3)

    pump(15)
    lower_far(15)

    @pl.when(is_mid)
    def _():
        raise_moved(3)
        lower_moved(5)

    last = 2 * per
    shared = [k for k in range(col) if k < per or k >= per + moved]
    for k in shared[:-1]:
        ret_copy(k).wait_recv()

    @pl.when(is_mid)
    def _():
        for k in range(per, last):
            ret_copy(k).wait_recv()

    @pl.when(is_end)
    def _():
        for j in range(per):
            for cross in range(2):
                moved_copy(j, cross).wait_recv()

    give((0, last), (last + 2, col - 1))
    raise_back(15)

    @pl.when(is_mid)
    def _():
        for h in range(HALVES):
            arrived(last, h).wait_recv()
        lower_moved(per)
        lower(last)

    ret_copy(15).wait_recv()
    give((col - 1, col))

    @pl.when(is_mid)
    def _():
        up_part(1).wait_recv()
        raise_moved(per + 1)
        raise_back(last + 1)
        up_part(0).wait_recv()
        raise_moved(per)
        raise_back(last)
        ret_copy(last + 1).wait_recv()
        ret_copy(last).wait_recv()

    @pl.when(is_end)
    def _():
        for j in (per + 1, per):
            for cross in range(2):
                moved_copy(j, cross).wait_recv()

    def finish(i, _):
        at = pl.ds(i * mt, mt)
        total = given(at, acc[at, :], ((last, last + 2),)) * scale_t[at, 0:1]
        c = cos_t[at, :]
        s = sin_t[at, :]
        for head in range(kv_local // HEAD):
            x = total[:, head * HEAD : (head + 1) * HEAD]
            r = x * c + pltpu.roll(x, HEAD // 2, 1) * s
            out[at, head * HEAD : (head + 1) * HEAD] = r.astype(jnp.bfloat16)
        out[at, kv_local:] = total[:, kv_local:].astype(jnp.bfloat16)
        pltpu.make_async_copy(out.at[at], out_hbm.at[at], out_sem.at[i]).start()
        return 0

    for i in range(rows // mt):
        finish(i, 0)

    for copy in sq_copies + base_copies:
        copy.wait_send()
    for l in range(per):
        for h in range(HALVES):
            own_send(l, h).wait_send()
    for k in range(col):
        y_copy(k).wait_send()

    def sent(k):
        ret_copy(k).wait_send()
        for m in range(1, tensors):
            low_copy(k, m).wait_send()

    for k in shared:
        sent(k)

    @pl.when(is_mid)
    def _():
        for k in forwarded:
            for h in range(HALVES):
                forward(k, h).wait_send()
        for q in (0, 2, 3):
            up_forward(q).wait_send()
        for n in range(3):
            up_part(n).wait_send()
        for k in range(per, per + moved):
            sent(k)
        for j in range(moved):
            for m in range(1, tensors):
                low_copy(col + j, m).wait_send()
            for cross in range(2):
                moved_copy(j, cross).wait_send()

    for i in range(rows // mt):
        at = pl.ds(i * mt, mt)
        pltpu.make_async_copy(out.at[at], out_hbm.at[at], out_sem.at[i]).wait()

    @pl.when(is_end)
    def _():
        up_send().wait_send()
        for j in range(moved):
            t_copy(j).wait_send()


def fused(
    tokens,
    norm_gain,
    kv_weight,
    adapter_down,
    adapter_up,
    token_adapters,
    adapter_slot,
    request_lengths,
):
    rows, width = tokens.shape
    capacity = max(2, 5 * rows // (4 * adapter_slot.shape[0]))
    cap = -(-capacity // 8) * 8
    stores = lax.axis_size("store")
    tensors = lax.axis_size("tensor")
    per, _, _, kv_local = adapter_up.shape
    depth = stores // 2
    col = depth * per
    moved = per + 2
    ranks = adapter_down.shape[2]
    vmem = pl.BlockSpec(memory_space=pltpu.VMEM)
    smem = pl.BlockSpec(memory_space=pltpu.SMEM)
    hbm = pl.BlockSpec(memory_space=pl.ANY)
    f32, bf16 = jnp.float32, jnp.bfloat16
    dma = pltpu.SemaphoreType.DMA
    both = pl.pallas_call(
        functools.partial(fused_kernel, stores, tensors, cap),
        out_shape=jax.ShapeDtypeStruct((rows, 2 * kv_local), bf16),
        in_specs=[vmem] * 2 + [smem] * 2 + [hbm] * 4,
        out_specs=hbm,
        scratch_shapes=[
            pltpu.VMEM((rows, 2 * kv_local), bf16),
            pltpu.VMEM((1, rows), jnp.int32),
            pltpu.VMEM((rows, 128), jnp.int32),
            pltpu.VMEM((rows, HEAD), f32),
            pltpu.VMEM((rows, HEAD), f32),
            pltpu.VMEM((rows, 128), f32),
            pltpu.VMEM((rows, width), bf16),
            pltpu.VMEM((2, 256, 2, kv_local * tensors), bf16),
            pltpu.VMEM((width, 2 * kv_local * tensors), bf16),
            pltpu.VMEM((col, width, ranks), bf16),
            pltpu.VMEM((depth, per, 2, ADAPTER_RANK, kv_local), bf16),
            pltpu.VMEM((col, 2, cap, width), bf16),
            pltpu.VMEM((col, cap, width), bf16),
            pltpu.VMEM((moved, 2, cap, width), bf16),
            pltpu.VMEM((8, rows), f32),
            pltpu.VMEM((tensors - 1, 8, rows), f32),
            pltpu.VMEM((rows, 2 * kv_local), f32),
            pltpu.VMEM((3, rows, 2 * kv_local), bf16),
            pltpu.VMEM((3, rows, 2 * kv_local), bf16),
            pltpu.VMEM((col + moved, 2 * cap, ranks), f32),
            pltpu.VMEM((col + moved, 2 * cap, ranks), bf16),
            pltpu.VMEM((tensors - 1, col + moved, 2 * cap, ranks), bf16),
            pltpu.VMEM((2 * col, cap, 2 * kv_local), bf16),
            pltpu.VMEM((col, cap, 2 * kv_local), bf16),
            pltpu.VMEM((moved, 2, cap, 2 * kv_local), bf16),
            dma((rows // 128,)),
            dma((2,)),
            dma((per,)),
            dma((1,)),
            dma((tensors - 1,)),
            dma((tensors - 1,)),
            dma((col,)),
            dma((col,)),
            dma((moved,)),
            dma((moved,)),
            dma((per, HALVES)),
            dma((col, HALVES)),
            dma((col, HALVES)),
            dma((2 + depth,)),
            dma((depth,)),
            dma((depth + 3,)),
            dma((3,)),
            dma((3,)),
            dma((col + moved, tensors - 1)),
            dma((col + moved, tensors - 1)),
            dma((col,)),
            dma((moved, 2)),
            dma((2 * col,)),
            dma((rows // 256,)),
            pltpu.SemaphoreType.REGULAR,
        ],
        compiler_params=pltpu.CompilerParams(
            collective_id=0, has_side_effects=True, vmem_limit_bytes=63 * 1024 * 1024
        ),
    )(
        norm_gain[None, :],
        token_adapters.reshape(1, rows),
        adapter_slot,
        request_lengths,
        tokens,
        adapter_up,
        kv_weight,
        adapter_down,
    )
    return both[:, :kv_local], both[:, kv_local:]


def local(
    tokens,
    norm_gain,
    kv_weight,
    adapter_down,
    adapter_up,
    token_adapters,
    adapter_slot,
    request_lengths,
):
    row_count = tokens.shape[0]
    local_width = tokens.shape[1]
    adapter_total = adapter_slot.shape[0]
    capacity = max(2, 5 * row_count // (4 * adapter_total))
    store_size = lax.axis_size("store")
    per_owner = adapter_down.shape[0]
    kv_local = adapter_up.shape[3]
    widened = tokens.astype(jnp.float32)
    squares = lax.psum(jnp.sum(widened * widened, axis=1), "tensor")
    normed = (widened * lax.rsqrt(squares / D + epsilon)[:, None] * norm_gain[None, :]).astype(
        jnp.bfloat16
    )
    targets = place_rows(token_adapters[:, 0], adapter_slot, capacity)
    send_rows = (
        jnp.zeros((adapter_total * capacity, local_width), jnp.bfloat16).at[targets].set(normed)
    )
    send_rows = send_rows.reshape(store_size, per_owner, capacity, local_width)
    down_projected = jnp.einsum(
        "slcd,ldr->slcr",
        lax.all_to_all(send_rows, "store", split_axis=0, concat_axis=0, tiled=True),
        adapter_down,
        preferred_element_type=jnp.float32,
    )
    rank_total_sum = lax.psum(down_projected, "tensor")
    rank_activation = (rank_total_sum * adapter_scale).astype(jnp.bfloat16)
    split_rank = rank_activation.reshape(rank_activation.shape[:3] + (2, ADAPTER_RANK))
    update_rows = jnp.einsum(
        "slcjr,ljrk->slcjk", split_rank, adapter_up, preferred_element_type=jnp.float32
    )
    back_rows = update_rows.astype(jnp.bfloat16).reshape(
        rank_activation.shape[:3] + (2 * kv_local,)
    )
    returned = lax.all_to_all(back_rows, "store", split_axis=0, concat_axis=0, tiled=True)
    delta_rows = returned.reshape(adapter_total * capacity, 2, kv_local)[targets]
    partial_value = jnp.einsum("td,djk->tjk", normed, kv_weight, preferred_element_type=jnp.float32)
    base_part = lax.psum_scatter(partial_value, "tensor", scatter_dimension=2, tiled=True)
    combined = base_part + delta_rows.astype(jnp.float32)
    positions = positions_of(lax.axis_index("store") * row_count, row_count, request_lengths)
    new_keys = rotate(combined[:, 0, :], positions).astype(jnp.bfloat16)
    new_values = combined[:, 1, :].astype(jnp.bfloat16)
    return (new_keys, new_values)


def solution(mesh):
    small = mesh.shape["store"] == 8 and mesh.shape["tensor"] == 4
    return jax.shard_map(
        fused if small else local,
        mesh=mesh,
        in_specs=(
            P("store", "tensor"),
            P("tensor"),
            P("tensor", None, None),
            P("store", "tensor", None),
            P("store", None, None, "tensor"),
            P("store", None),
            P(),
            P(),
        ),
        out_specs=(P("store", "tensor"), P("store", "tensor")),
        check_vma=False,
    )
```
